32 devices in a mesh: fsdp: 4 (over z), ctx: 4 (over y, core), tp: 2 (over x).
Axes of the slice: x: 2, y: 2, z: 4, core: 2. Of those that a mesh axis runs over, the one named last changes fastest.
Arguments:
- prompt_x: bfloat16 [4, 1024, 2304], P('fsdp', 'ctx'), may hold values from -6 to 6
- cont_x: bfloat16 [16, 256, 2304], P(('fsdp', 'ctx')), may hold values from -6 to 6
- cont_prompt: int32 [16], P(('fsdp', 'ctx')), may hold values from 0 to 3, as said below
- cont_len: int32 [16], P(('fsdp', 'ctx')), may hold values from 64 to 256, as said below
- attn_norm: bfloat16 [2304], P(('fsdp', 'ctx')), may hold values from 0.25 to 1.75
- attn_post: bfloat16 [2304], P(('fsdp', 'ctx')), may hold values from 0.25 to 1.75
- mlp_norm: bfloat16 [2304], P(('fsdp', 'ctx')), may hold values from 0.25 to 1.75
- mlp_post: bfloat16 [2304], P(('fsdp', 'ctx')), may hold values from 0.25 to 1.75
- w_query: bfloat16 [2304, 2048], P(('fsdp', 'ctx'), 'tp'), may hold values from -0.125 to 0.125
- w_key: bfloat16 [2304, 1024], P(('fsdp', 'ctx'), 'tp'), may hold values from -0.125 to 0.125
- w_value: bfloat16 [2304, 1024], P(('fsdp', 'ctx'), 'tp'), may hold values from -0.125 to 0.125
- w_out: bfloat16 [2048, 2304], P('tp', ('fsdp', 'ctx')), may hold values from -0.125 to 0.125
- w_gate: bfloat16 [2304, 9216], P(('fsdp', 'ctx'), 'tp'), may hold values from -0.125 to 0.125
- w_up: bfloat16 [2304, 9216], P(('fsdp', 'ctx'), 'tp'), may hold values from -0.125 to 0.125
- w_down: bfloat16 [9216, 2304], P('tp', ('fsdp', 'ctx')), may hold values from -0.0625 to 0.0625
- prompt_cot: bfloat16 [4, 1024, 2304], P('fsdp', 'ctx'), may hold values from -6 to 6
- cont_cot: bfloat16 [16, 256, 2304], P(('fsdp', 'ctx')), may hold values from -6 to 6
Outputs:
- y_prompt: bfloat16 [4, 1024, 2304], P('fsdp', 'ctx')
- y_cont: bfloat16 [16, 256, 2304], P(('fsdp', 'ctx'))
- grad_prompt: float32 [4, 1024, 2304], P('fsdp', 'ctx')
- grad_cont: float32 [16, 256, 2304], P(('fsdp', 'ctx'))
- grad_attn_norm: float32 [2304], P(('fsdp', 'ctx'))
- grad_attn_post: float32 [2304], P(('fsdp', 'ctx'))
- grad_mlp_norm: float32 [2304], P(('fsdp', 'ctx'))
- grad_mlp_post: float32 [2304], P(('fsdp', 'ctx'))
- grad_w_query: float32 [2304, 2048], P(('fsdp', 'ctx'), 'tp')
- grad_w_key: float32 [2304, 1024], P(('fsdp', 'ctx'), 'tp')
- grad_w_value: float32 [2304, 1024], P(('fsdp', 'ctx'), 'tp')
- grad_w_out: float32 [2048, 2304], P('tp', ('fsdp', 'ctx'))
- grad_w_gate: float32 [2304, 9216], P(('fsdp', 'ctx'), 'tp')
- grad_w_up: float32 [2304, 9216], P(('fsdp', 'ctx'), 'tp')
- grad_w_down: float32 [9216, 2304], P('tp', ('fsdp', 'ctx'))
The draws below stay inside these ranges and needn't reach their ends.
Inputs may be any that keep to these rules, and one draw needn't show every extreme that they name: `cont_prompt`: each of the 4 prompts is continued by the same number of continuations. `cont_len`: some continuation is live in all 256 positions.
All inputs are finite; a program needn't handle non-finite values.
Results may differ from the reference program's by a relative error of at most 0.018.
Values may be sent and summed in bfloat16 or wider, within the bound.
No kernel may reach another device: no remote copies, remote signals or barrier semaphores. Data moves between devices by JAX's collectives and lax.ppermute only.
A program may use at most 384 MiB of HBM per device.

```python
import math
import jax
import jax.numpy as jnp
from jax import lax

D = 2304
H = 8
KVH = 4
HD = 256
FF = 9216
PROMPT = 1024
CLEN = 256
GROUPS = 4
NCONT = 16


def draw_cont_prompt(key, part):
    shuffled = jax.random.permutation(key, NCONT)
    return (shuffled % GROUPS).astype(jnp.int32)


def draw_cont_len(key, part):
    key_lens, key_pick = jax.random.split(key)
    lengths = jax.random.randint(key_lens, (NCONT,), CLEN // 4, CLEN + 1)
    chosen = jax.random.randint(key_pick, (), 0, NCONT)
    return jnp.where(jnp.arange(NCONT) == chosen, CLEN, lengths).astype(jnp.int32)


def spiked(entries, rng, source, target, shards_of, factor):
    def block_of(axis_at):
        return (jnp.arange(entries.shape[axis_at]) // (entries.shape[axis_at] // shards_of)).reshape((-1,) + (1,) * (entries.ndim - 1 - axis_at))

    first = jax.random.permutation(rng, shards_of)[block_of(target)]
    other_side = (block_of(target) + shards_of // 2) % shards_of
    return jnp.where((block_of(source) == first) | (block_of(source) == other_side), factor * entries, entries)


def shard_levels(key, shape, shards, low, largest):
    level = 1.0
    for position, blocks in shards:
        draws = jax.random.uniform(jax.random.fold_in(jax.random.fold_in(key, 6), position), (blocks,), jnp.float32, low / len(shards), largest / len(shards))
        level = level * jnp.repeat(jnp.exp(draws), shape[position] // blocks).reshape((-1,) + (1,) * (len(shape) - 1 - position))
    return level


def scatter_about(stream_key, extent, width, reach, cuts=(), kind=jnp.bfloat16):
    loudness = shard_levels(stream_key, extent, cuts, -0.22, 0.18) if cuts else 1.0
    values = jax.random.normal(stream_key, extent, jnp.float32) * width * loudness
    return jnp.minimum(jnp.maximum(values, -reach), reach).astype(kind)


def bell_draw_with(rng, shape, deviation, limit, pieces, heavy, kind=jnp.bfloat16):
    values = deviation * jax.random.normal(rng, shape, jnp.float32)
    if pieces:
        values = values * shard_levels(rng, shape, pieces, -0.22, 0.18)
    return jnp.clip(spiked(values, jax.random.fold_in(rng, 3), *heavy), -limit, limit).astype(kind)


def setup_inputs(seed: int = 0) -> dict:
    key_of = jax.random.split(jax.random.key(seed), 18)
    return {
        "prompt_x": scatter_about(key_of[0], (GROUPS, PROMPT, D), 1.0, 6.0, ((0, 4), (1, 4))),
        "cont_x": scatter_about(key_of[1], (NCONT, CLEN, D), 1.0, 6.0, ((0, 16),)),
        "cont_prompt": draw_cont_prompt(jax.random.fold_in(key_of[17], 71), 0),
        "cont_len": draw_cont_len(jax.random.fold_in(key_of[17], 71), 0),
        "attn_norm": jnp.clip(1.0 + 0.15 * jax.random.normal(key_of[4], (D,), jnp.float32), 0.25, 1.75).astype(jnp.bfloat16),
        "attn_post": jnp.clip(1.0 + 0.15 * jax.random.normal(key_of[5], (D,), jnp.float32), 0.25, 1.75).astype(jnp.bfloat16),
        "mlp_norm": jnp.clip(1.0 + 0.15 * jax.random.normal(key_of[6], (D,), jnp.float32), 0.25, 1.75).astype(jnp.bfloat16),
        "mlp_post": jnp.clip(1.0 + 0.15 * jax.random.normal(key_of[7], (D,), jnp.float32), 0.25, 1.75).astype(jnp.bfloat16),
        "w_query": scatter_about(key_of[8], (D, H * HD), D ** -0.5, 0.125, ((0, 16), (1, 2))),
        "w_key": scatter_about(key_of[9], (D, KVH * HD), D ** -0.5, 0.125, ((0, 16), (1, 2))),
        "w_value": scatter_about(key_of[10], (D, KVH * HD), D ** -0.5, 0.125, ((0, 16), (1, 2))),
        "w_out": scatter_about(key_of[11], (H * HD, D), (H * HD) ** -0.5, 0.125, ((0, 2), (1, 16))),
        "w_gate": scatter_about(key_of[12], (D, FF), D ** -0.5, 0.125, ((0, 16), (1, 2))),
        "w_up": scatter_about(key_of[13], (D, FF), D ** -0.5, 0.125, ((0, 16), (1, 2))),
        "w_down": scatter_about(key_of[14], (FF, D), FF ** -0.5, 0.0625, ((0, 2), (1, 16))),
        "prompt_cot": scatter_about(key_of[15], (GROUPS, PROMPT, D), 1.0, 6.0, ((0, 4), (1, 4))),
        "cont_cot": bell_draw_with(key_of[16], (NCONT, CLEN, D), 1.0, 6.0, ((0, 16),), (0, 2, 16, 2.0)),
    }


@jax.custom_vjp
def low(v):
    return lax.optimization_barrier(v.astype(jnp.bfloat16)).astype(jnp.float32)

@jax.custom_vjp
def low_back(v):
    return v

def low_keep(v):
    return (low(v), None)

def low_pass(kept, grad):
    return (grad,)

def back_keep(v):
    return (v, None)

def back_low(kept, grad):
    return (low(grad),)
low.defvjp(low_keep, low_pass)
low_back.defvjp(back_keep, back_low)
soft_cap = 50.0
norm_eps = 1e-06
strict_precision = lax.Precision.HIGHEST

def matmul(left, right):
    return jnp.dot(left, right, precision=strict_precision)

def rms_norm(values, scales):
    return values * lax.rsqrt(lax.optimization_barrier(jnp.mean(values * values, axis=-1, keepdims=True)) + norm_eps) * scales

def rotary(values, places):
    half_dim = values.shape[-1] // 2
    frequency = jnp.exp(jnp.arange(half_dim, dtype=jnp.float32) * (-2.0 * math.log(10000.0) / values.shape[-1]))
    angles = places[:, None] * frequency[None, :]
    cosine = jnp.cos(angles)[:, None, :]
    sine_wave = jnp.sin(angles)[:, None, :]
    front_half = values[..., :half_dim]
    back_half = values[..., half_dim:]
    return jnp.concatenate([front_half * cosine - back_half * sine_wave, back_half * cosine + front_half * sine_wave], axis=-1)

def attend(query_matrix, key_rows, value_rows, allowed):
    shared_by = query_matrix.shape[1] // key_rows.shape[1]
    repeated_keys = jnp.repeat(key_rows, shared_by, axis=1)
    repeated_values = jnp.repeat(value_rows, shared_by, axis=1)
    logit_scores = low_back(jnp.einsum('kqx,wqx->qkw', query_matrix, repeated_keys, precision=strict_precision))
    capped = soft_cap * jnp.tanh(logit_scores / soft_cap)
    capped = jnp.where(allowed[None], capped, -1e+30)
    weight_set = low(jax.nn.softmax(capped, axis=-1))
    return jnp.einsum('vib,bvo->ivo', weight_set, repeated_values, precision=strict_precision)

def forward(prompt_x, cont_x, attn_norm, attn_post, mlp_norm, mlp_post, w_query, w_key, w_value, w_out, w_gate, w_up, w_down, cont_prompt, cont_len):
    prompt_rows = GROUPS * PROMPT
    total_rows = prompt_rows + NCONT * CLEN
    hidden_in = jnp.concatenate([prompt_x.reshape(prompt_rows, D), cont_x.reshape(NCONT * CLEN, D)], axis=0)
    places = jnp.concatenate([jnp.tile(jnp.arange(PROMPT, dtype=jnp.int32), GROUPS), PROMPT + jnp.tile(jnp.arange(CLEN, dtype=jnp.int32), NCONT)]).astype(jnp.float32)
    normed = low(rms_norm(hidden_in, attn_norm))
    query_proj = low_back(matmul(normed, w_query))
    key_proj = low_back(matmul(normed, w_key))
    value_all = low_back(low(matmul(normed, w_value))).reshape(total_rows, KVH, HD)
    query_all = low(rotary(query_proj.reshape(total_rows, H, HD), places) * HD ** (-0.5))
    key_all = low(rotary(key_proj.reshape(total_rows, KVH, HD), places))
    prompt_query = query_all[:prompt_rows].reshape(GROUPS, PROMPT, H, HD)
    prompt_key = key_all[:prompt_rows].reshape(GROUPS, PROMPT, KVH, HD)
    prompt_value = value_all[:prompt_rows].reshape(GROUPS, PROMPT, KVH, HD)
    causal = jnp.arange(PROMPT, dtype=jnp.int32)[None, :] <= jnp.arange(PROMPT, dtype=jnp.int32)[:, None]

    def prompt_block(operands):
        return attend(operands[0], operands[1], operands[2], causal)
    prompt_mixed = lax.map(jax.checkpoint(prompt_block), (prompt_query, prompt_key, prompt_value))
    cont_query = query_all[prompt_rows:].reshape(NCONT, CLEN, H, HD)
    cont_key = key_all[prompt_rows:].reshape(NCONT, CLEN, KVH, HD)
    cont_value = value_all[prompt_rows:].reshape(NCONT, CLEN, KVH, HD)
    cont_allowed = jnp.arange(PROMPT + CLEN, dtype=jnp.int32)[None, :] <= PROMPT + jnp.arange(CLEN, dtype=jnp.int32)[:, None]

    def cont_block(operands):
        own_query, own_key, own_value, owner_id = operands
        seen_key = jnp.concatenate([prompt_key[owner_id], own_key], axis=0)
        seen_value = jnp.concatenate([prompt_value[owner_id], own_value], axis=0)
        return attend(own_query, seen_key, seen_value, cont_allowed)
    cont_mixed = lax.map(jax.checkpoint(cont_block), (cont_query, cont_key, cont_value, cont_prompt))
    attn_out = jnp.concatenate([prompt_mixed.reshape(prompt_rows, H * HD), cont_mixed.reshape(NCONT * CLEN, H * HD)], axis=0)
    attn_out = low_back(low(attn_out))
    branch = low_back(matmul(attn_out, w_out))
    middle = hidden_in + rms_norm(branch, attn_post)
    cont_live = (jnp.arange(CLEN, dtype=jnp.int32)[None, :] < cont_len[:, None]).astype(jnp.float32).reshape(NCONT * CLEN)
    live_all = jnp.concatenate([jnp.ones((prompt_rows,), jnp.float32), cont_live])

    def mlp_block(operands):
        mid_rows, live_rows = operands
        mlp_in = low(rms_norm(mid_rows, mlp_norm))
        gate_proj = low_back(matmul(mlp_in, w_gate))
        up_proj = low_back(matmul(mlp_in, w_up))
        inner_act = low(jax.nn.gelu(gate_proj, approximate=True) * up_proj)
        mlp_out = low_back(matmul(inner_act, w_down))
        return (mid_rows + rms_norm(mlp_out, mlp_post)) * live_rows[:, None]
    block_rows = math.gcd(total_rows, 4096)
    result = lax.map(jax.checkpoint(mlp_block), (middle.reshape(total_rows // block_rows, block_rows, D), live_all.reshape(total_rows // block_rows, block_rows)))
    result = result.reshape(total_rows, D)
    return (result[:prompt_rows].reshape(GROUPS, PROMPT, D), result[prompt_rows:].reshape(NCONT, CLEN, D))

def reference(prompt_x, cont_x, cont_prompt, cont_len, attn_norm, attn_post, mlp_norm, mlp_post, w_query, w_key, w_value, w_out, w_gate, w_up, w_down, prompt_cot, cont_cot):
    floats = (prompt_x, cont_x, attn_norm, attn_post, mlp_norm, mlp_post, w_query, w_key, w_value, w_out, w_gate, w_up, w_down)
    floats = tuple((array_in.astype(jnp.float32) for array_in in floats))

    def wrapped(*arrays):
        return forward(*arrays, cont_prompt, cont_len)
    primal, pullback = jax.vjp(wrapped, *floats)
    gradients = pullback((prompt_cot.astype(jnp.float32), cont_cot.astype(jnp.float32)))
    return (primal[0].astype(jnp.bfloat16), primal[1].astype(jnp.bfloat16), gradients[0], gradients[1], gradients[2], gradients[3], gradients[4], gradients[5], gradients[6], gradients[7], gradients[8], gradients[9], gradients[10], gradients[11], gradients[12])
```

```python
import math

import jax
import jax.numpy as jnp
from jax import lax
from jax.sharding import PartitionSpec as P

HD = 256
PROMPT = 1024

soft_cap = 50.0
norm_eps = 1e-06
masked_fill = -1e30
bf16 = jnp.bfloat16
f32 = jnp.float32


def norm_parts(values):
    inverse = lax.rsqrt(jnp.mean(values * values, axis=-1, keepdims=True) + norm_eps)
    return (values * inverse, inverse)


def norm_back(grad_normal, normal, inverse):
    return inverse * (
        grad_normal - normal * jnp.mean(grad_normal * normal, axis=-1, keepdims=True)
    )


def rotary_tables(places, head_dim):
    half_dim = head_dim // 2
    frequency = jnp.exp(
        jnp.arange(half_dim, dtype=f32) * (-2.0 * math.log(10000.0) / head_dim)
    )
    angles = places[:, None] * frequency[None, :]
    return (jnp.cos(angles), jnp.sin(angles))


def rotary(values, cosine, sine_wave):
    half_dim = values.shape[-1] // 2
    front_half = values[..., :half_dim]
    back_half = values[..., half_dim:]
    return jnp.concatenate(
        [front_half * cosine - back_half * sine_wave, back_half * cosine + front_half * sine_wave],
        axis=-1,
    )


def matmul(left, right):
    return jnp.dot(left, right, preferred_element_type=f32)


def matmul_rt(left, right):
    return lax.dot_general(left, right, (((1,), (1,)), ((), ())), preferred_element_type=f32)


def matmul_lt(left, right):
    return lax.dot_general(left, right, (((0,), (0,)), ((), ())), preferred_element_type=f32)


def attend_forward(query, key, value, allowed):
    raw_scores = matmul_rt(query, key)
    capped = jnp.where(allowed, soft_cap * jnp.tanh(raw_scores / soft_cap), masked_fill)
    row_peak = jnp.max(capped, axis=-1, keepdims=True)
    exponent = jnp.exp(capped - row_peak)
    row_total = jnp.sum(exponent, axis=-1, keepdims=True)
    weight_set = (exponent / row_total).astype(bf16)
    return (matmul(weight_set, value), row_peak + jnp.log(row_total))


def attend_backward(query, key, value, allowed, log_total, grad_mixed):
    raw_scores = matmul_rt(query, key)
    squashed = jnp.tanh(raw_scores / soft_cap)
    capped = jnp.where(allowed, soft_cap * squashed, masked_fill)
    probabilities = jnp.exp(capped - log_total)
    weight_set = probabilities.astype(bf16)
    grad_value = matmul_lt(weight_set, grad_mixed)
    grad_probs = matmul_rt(grad_mixed, value)
    inner_sum = jnp.sum(probabilities * grad_probs, axis=-1, keepdims=True)
    grad_scores = (probabilities * (grad_probs - inner_sum) * (1.0 - squashed * squashed)).astype(
        bf16
    )
    return (matmul(grad_scores, key), matmul_lt(grad_scores, query), grad_value)


def shards(
    prompt_x,
    cont_x,
    cont_prompt,
    cont_len,
    attn_norm,
    attn_post,
    mlp_norm,
    mlp_post,
    w_query,
    w_key,
    w_value,
    w_out,
    w_gate,
    w_up,
    w_down,
    prompt_cot,
    cont_cot,
):
    width = prompt_x.shape[2]
    prompt_local = prompt_x.shape[1]
    cont_count = cont_x.shape[0]
    cont_size = cont_x.shape[1]
    cont_rows = cont_count * cont_size
    rows = prompt_local + cont_rows
    z_size = lax.axis_size("fsdp")
    c_size = lax.axis_size("ctx")
    y_size = c_size // 2
    z = lax.axis_index("fsdp")
    c = lax.axis_index("ctx")
    y = c // 2
    core = c % 2
    t = lax.axis_index("tp")
    part = w_query.shape[0]
    q_cols = w_query.shape[1] // 2
    kv_cols = w_key.shape[1] // 2
    shared_by = q_cols // kv_cols
    a_cols = q_cols + 2 * kv_cols
    block = w_gate.shape[1] // z_size
    share = rows // 2
    query_scale = HD ** (-0.5)

    def z_shift(values, step):
        return lax.ppermute(values, "fsdp", [(i, (i + step) % z_size) for i in range(z_size)])

    def y_next(values):
        return lax.ppermute(values, "ctx", [(i, (i + 2) % c_size) for i in range(c_size)])

    def core_swap(values):
        return lax.ppermute(values, "ctx", [(i, i ^ 1) for i in range(c_size)])

    def tp_swap(values):
        return lax.ppermute(values, "tp", [(0, 1), (1, 0)])

    def by_core(own, other):
        return (jnp.where(core == 0, own, other), jnp.where(core == 0, other, own))

    def gather_grid(own):
        held = jnp.zeros((z_size, y_size) + own.shape, own.dtype)
        tail = (0,) * own.ndim
        chunk = own
        for step in range(z_size):
            if step:
                chunk = z_shift(chunk, 1)
            turn = chunk
            for hop in range(y_size):
                if hop:
                    turn = y_next(turn)
                held = lax.dynamic_update_slice(
                    held,
                    turn[None, None],
                    ((z - step) % z_size, (y - hop) % y_size) + tail,
                )
        return held

    def scatter_grid(take):
        sums = {}
        for step in list(range(1, z_size)) + [0]:
            to_z = (z - step) % z_size
            total = take(to_z, (y - 1) % y_size)
            for hop in range(2, y_size + 1):
                total = y_next(total.astype(bf16)).astype(f32) + take(to_z, (y - hop) % y_size)
            sums[step] = total
        total = sums[1]
        for step in list(range(2, z_size)) + [0]:
            total = z_shift(total.astype(bf16), 1).astype(f32) + sums[step]
        return total

    def taker(values):
        tail = (0,) * (values.ndim - 2)

        def take(z_at, y_at):
            piece = lax.dynamic_slice(values, (z_at, y_at) + tail, (1, 1) + values.shape[2:])
            return piece[0, 0].astype(f32)

        return take

    def take_share(values):
        return lax.dynamic_slice_in_dim(values, t * share, share, 0)

    def give_share(values):
        return lax.dynamic_slice_in_dim(values, (1 - t) * share, share, 0)

    def rows_of(mine, other):
        return jnp.concatenate(
            [jnp.where(t == 0, mine, other), jnp.where(t == 0, other, mine)], axis=0
        )

    gain_one = attn_norm.astype(f32)[:, None]
    gain_three = mlp_norm.astype(f32)[:, None]
    scaled_q = (w_query.astype(f32) * gain_one).astype(bf16)
    scaled_k = (w_key.astype(f32) * gain_one).astype(bf16)
    scaled_v = (w_value.astype(f32) * gain_one).astype(bf16)

    def head_cols(which):
        return jnp.concatenate(
            [
                lax.dynamic_slice_in_dim(scaled_q, which * q_cols, q_cols, 1),
                lax.dynamic_slice_in_dim(scaled_k, which * kv_cols, kv_cols, 1),
                lax.dynamic_slice_in_dim(scaled_v, which * kv_cols, kv_cols, 1),
            ],
            axis=1,
        )

    mine, other = by_core(head_cols(core), core_swap(head_cols(1 - core)))
    attn_w = gather_grid(jnp.stack([mine, other], axis=0)).reshape(width, a_cols)

    post_low = jnp.zeros((1, 8, 256), bf16)
    post_low = post_low.at[0, 0, :part].set(attn_post).at[0, 1, :part].set(mlp_post)
    post_all = lax.all_gather(post_low, ("fsdp", "ctx"), axis=0, tiled=True)
    post_attn = post_all[:, 0, :part].reshape(1, width).astype(f32)
    post_mlp = post_all[:, 1, :part].reshape(1, width).astype(f32)

    residual = jnp.concatenate(
        [prompt_x.reshape(prompt_local, width), cont_x.reshape(cont_rows, width)], axis=0
    ).astype(f32)
    normal_one, inverse_one = norm_parts(residual)
    normal_low = normal_one.astype(bf16)
    chip_rows = jnp.concatenate([normal_low, core_swap(normal_low)], axis=0)

    out_t = w_out.T
    mine, other = by_core(
        lax.dynamic_slice_in_dim(out_t, core * q_cols, q_cols, 1),
        core_swap(lax.dynamic_slice_in_dim(out_t, (1 - core) * q_cols, q_cols, 1)),
    )
    out_w = gather_grid(jnp.stack([mine, other], axis=0)).reshape(width, q_cols)

    def mlp_weight(local):
        blocks = local.reshape(part, z_size, block)
        held = jnp.zeros((z_size, part, block), bf16)
        for step in range(z_size):
            piece = lax.dynamic_slice_in_dim(local, ((z + step) % z_size) * block, block, 1)
            if step:
                piece = z_shift(piece, step)
            held = lax.dynamic_update_slice(held, piece[None], ((z - step) % z_size, 0, 0))
        del blocks
        full = jnp.zeros((z_size, y_size, 2, part, block), bf16)
        turn = held
        for hop in range(y_size):
            if hop:
                turn = y_next(turn)
            cross = tp_swap(turn)
            keep = jnp.where(t == core, turn, cross)
            give = jnp.where(t == core, cross, turn)
            got = core_swap(give)
            y_at = (y - hop) % y_size
            full = lax.dynamic_update_slice(full, keep[:, None, None], (0, y_at, core, 0, 0))
            full = lax.dynamic_update_slice(full, got[:, None, None], (0, y_at, 1 - core, 0, 0))
        return full.reshape(width, block)

    gate_w = mlp_weight((w_gate.astype(f32) * gain_three).astype(bf16))
    up_w = mlp_weight((w_up.astype(f32) * gain_three).astype(bf16))
    down_w = mlp_weight(w_down.T)

    core_of = (core, 1 - core)
    cont_places = PROMPT + jnp.tile(jnp.arange(cont_size, dtype=jnp.int32), cont_count)
    prompt_places = [
        (y * 2 + which) * prompt_local + jnp.arange(prompt_local, dtype=jnp.int32)
        for which in core_of
    ]
    places = jnp.concatenate(
        [prompt_places[0], cont_places, prompt_places[1], cont_places]
    ).astype(f32)
    cosine, sine_wave = rotary_tables(places, HD)
    projected = matmul(chip_rows, attn_w)
    query_rows = jnp.stack(
        [
            (rotary(projected[:, i * HD : (i + 1) * HD], cosine, sine_wave) * query_scale).astype(bf16)
            for i in range(shared_by)
        ],
        axis=0,
    ).reshape(shared_by, 2, rows, HD)
    key_rows = rotary(projected[:, q_cols : q_cols + HD], cosine, sine_wave).astype(bf16)
    value_rows = projected[:, q_cols + HD :].astype(bf16)
    kv_rows = jnp.concatenate([key_rows, value_rows], axis=1).reshape(2, rows, 2 * HD)
    prompt_kv = kv_rows[:, :prompt_local].reshape(2 * prompt_local, 2 * HD)
    every_kv = gather_grid(prompt_kv).reshape(z_size, y_size * 2 * prompt_local, 2 * HD)
    span = every_kv.shape[1]
    own_kv = lax.dynamic_slice(every_kv, (z, 0, 0), (1, span, 2 * HD))[0]
    key_places = (
        (jnp.arange(y_size, dtype=jnp.int32)[:, None, None] * 2
         + jnp.stack(core_of)[None, :, None]) * prompt_local
        + jnp.arange(prompt_local, dtype=jnp.int32)[None, None, :]
    ).reshape(1, span)
    head_places = jnp.tile(jnp.concatenate(prompt_places), shared_by)
    prompt_allowed = key_places <= head_places[:, None]
    cont_allowed = jnp.tile(
        jnp.arange(span + cont_size, dtype=jnp.int32)[None, :]
        <= span + jnp.arange(cont_size, dtype=jnp.int32)[:, None],
        (shared_by, 1),
    )
    prompt_query = query_rows[:, :, :prompt_local].reshape(-1, HD)
    prompt_mixed, prompt_total = attend_forward(
        prompt_query, own_kv[:, :HD], own_kv[:, HD:], prompt_allowed
    )
    prompt_mixed = prompt_mixed.astype(bf16).reshape(shared_by, 2, prompt_local, HD)
    other_prompt = core_swap(cont_prompt)
    which_prompt = [cont_prompt[i] for i in range(cont_count)] + [
        other_prompt[i] for i in range(cont_count)
    ]
    conts = []
    for i in range(2 * cont_count):
        at = prompt_local + (i % cont_count) * cont_size
        half = i // cont_count
        kv = jnp.concatenate(
            [
                lax.dynamic_slice(every_kv, (which_prompt[i], 0, 0), (1, span, 2 * HD))[0],
                kv_rows[half, at : at + cont_size],
            ],
            axis=0,
        )
        query = query_rows[:, half, at : at + cont_size].reshape(-1, HD)
        mixed, total = attend_forward(query, kv[:, :HD], kv[:, HD:], cont_allowed)
        conts.append((query, kv, mixed.astype(bf16).reshape(shared_by, cont_size, HD), total))

    def rows_order(prompt_part, cont_parts):
        halves = []
        for half in range(2):
            pieces = [prompt_part[:, half]] + cont_parts[half * cont_count : (half + 1) * cont_count]
            halves.append(jnp.concatenate(pieces, axis=1))
        heads = jnp.concatenate(halves, axis=1)
        return jnp.concatenate([heads[i] for i in range(shared_by)], axis=1)

    attn_out = rows_order(prompt_mixed, [entry[2] for entry in conts])

    def to_shares(partial):
        low = partial.astype(bf16)
        summed = partial[:rows] + core_swap(low[rows:]).astype(f32)
        return take_share(summed) + tp_swap(give_share(summed).astype(bf16)).astype(f32)

    branch = to_shares(matmul_rt(attn_out, out_w))

    normal_two, inverse_two = norm_parts(branch)
    middle = take_share(residual) + normal_two * post_attn
    normal_three, inverse_three = norm_parts(middle)

    def ring_rows(own, step_fn):
        sums = []
        chunk = own
        for step in range(z_size):
            if step:
                chunk = z_shift(chunk, 1)
            both = jnp.concatenate([chunk, core_swap(chunk)], axis=0)
            partial = step_fn(step, both)
            sums.append(
                partial[:share] + core_swap(partial[share:].astype(bf16)).astype(f32)
            )
        total = sums[1]
        for step in list(range(2, z_size)) + [0]:
            total = z_shift(total.astype(bf16), 1).astype(f32) + sums[step]
        return total

    mlp_in, gates, ups, inners = {}, {}, {}, {}

    def mlp_forward(step, both):
        mlp_in[step] = both
        gates[step] = matmul(both, gate_w)
        ups[step] = matmul(both, up_w)
        inners[step] = (jax.nn.gelu(gates[step], approximate=True) * ups[step]).astype(bf16)
        return matmul_rt(inners[step], down_w)

    mlp_share = ring_rows(normal_three.astype(bf16), mlp_forward)

    normal_four, inverse_four = norm_parts(mlp_share)
    cont_live = (
        (jnp.arange(cont_size, dtype=jnp.int32)[None, :] < cont_len[:, None])
        .astype(f32)
        .reshape(cont_rows)
    )
    live_rows = jnp.concatenate([jnp.ones((prompt_local,), f32), cont_live])
    live = take_share(live_rows)[:, None]
    result_share = ((middle + normal_four * post_mlp) * live).astype(bf16)
    result_rows = rows_of(result_share, tp_swap(result_share))
    cot_rows = jnp.concatenate(
        [prompt_cot.reshape(prompt_local, width), cont_cot.reshape(cont_rows, width)], axis=0
    )
    grad_result = take_share(cot_rows).astype(f32) * live
    grad_post_mlp = jnp.sum(grad_result * normal_four, axis=0)
    grad_mlp = norm_back(grad_result * post_mlp, normal_four, inverse_four)

    grad_outs, grad_gates, grad_ups = {}, {}, {}

    def mlp_backward(step, both):
        grad_outs[step] = both
        grad_inner = matmul(both, down_w)
        pull = jax.vjp(
            lambda gate_in, up_in: jax.nn.gelu(gate_in, approximate=True) * up_in,
            gates[step],
            ups[step],
        )[1]
        grad_gate, grad_up = pull(grad_inner)
        grad_gates[step] = grad_gate.astype(bf16)
        grad_ups[step] = grad_up.astype(bf16)
        return matmul_rt(grad_gates[step], gate_w) + matmul_rt(grad_ups[step], up_w)

    grad_three = ring_rows(grad_mlp.astype(bf16), mlp_backward)

    def joined(pieces):
        return jnp.concatenate([pieces[step] for step in range(z_size)], axis=0)

    all_in, all_grad = joined(mlp_in), joined(grad_outs)
    grad_down_w = matmul_lt(all_grad, joined(inners)).astype(bf16)
    grad_gate_w = matmul_lt(all_in, joined(grad_gates)).astype(bf16)
    grad_up_w = matmul_lt(all_in, joined(grad_ups)).astype(bf16)

    def mlp_grad(full):
        full = full.reshape(z_size, y_size, 2, part, block)

        def of_core(which):
            return lax.dynamic_slice(
                full, (0, 0, which, 0, 0), (z_size, y_size, 1, part, block)
            )[:, :, 0]

        mine, got = of_core(core), core_swap(of_core(1 - core))
        keep = jnp.where(t == core, mine, got).astype(f32)
        summed = keep + tp_swap(jnp.where(t == core, got, mine)).astype(f32)

        def y_term(at):
            return lax.dynamic_slice(summed, (0, at, 0, 0), (z_size, 1, part, block))[:, 0]

        total = y_term((y - 1) % y_size)
        for hop in range(2, y_size + 1):
            total = y_next(total.astype(bf16)).astype(f32) + y_term((y - hop) % y_size)
        low = total.astype(bf16)
        held = jnp.zeros((part, z_size * block), bf16)
        for step in range(z_size):
            piece = lax.dynamic_slice_in_dim(low, (z + step) % z_size, 1, 0)[0]
            if step:
                piece = z_shift(piece, step)
            held = lax.dynamic_update_slice(held, piece, (0, ((z - step) % z_size) * block))
        return held.astype(f32)

    raw_down = mlp_grad(grad_down_w)
    raw_gate = mlp_grad(grad_gate_w)
    raw_up = mlp_grad(grad_up_w)

    grad_middle = grad_result + norm_back(grad_three, normal_three, inverse_three)
    grad_post_attn = jnp.sum(grad_middle * normal_two, axis=0)
    grad_branch = norm_back(grad_middle * post_attn, normal_two, inverse_two).astype(bf16)
    branch_rows = rows_of(grad_branch, tp_swap(grad_branch))
    branch_chip = jnp.concatenate([branch_rows, core_swap(branch_rows)], axis=0)
    grad_attn = matmul(branch_chip, out_w).astype(bf16)
    grad_out_w = matmul_lt(branch_chip, attn_out).astype(bf16)
    post_terms = jnp.stack([grad_post_attn, grad_post_mlp], axis=1).astype(bf16)
    grad_out_w = jnp.concatenate(
        [grad_out_w, post_terms, jnp.zeros((width, 126), bf16)], axis=1
    ).reshape(z_size, y_size, 2 * part, q_cols + 128)
    out_sum = scatter_grid(taker(grad_out_w))

    grad_heads = jnp.stack(
        [grad_attn[:, i * HD : (i + 1) * HD] for i in range(shared_by)], axis=0
    ).reshape(shared_by, 2, rows, HD)
    prompt_gq, prompt_gk, prompt_gv = attend_backward(
        prompt_query,
        own_kv[:, :HD],
        own_kv[:, HD:],
        prompt_allowed,
        prompt_total,
        grad_heads[:, :, :prompt_local].reshape(-1, HD),
    )
    prompt_gkv = jnp.concatenate([prompt_gk, prompt_gv], axis=1)
    cont_gq, cont_gkv, own_gkv = [], [], []
    for i in range(2 * cont_count):
        at = prompt_local + (i % cont_count) * cont_size
        half = i // cont_count
        query, kv, _, total = conts[i]
        gq, gk, gv = attend_backward(
            query,
            kv[:, :HD],
            kv[:, HD:],
            cont_allowed,
            total,
            grad_heads[:, half, at : at + cont_size].reshape(-1, HD),
        )
        cont_gq.append(gq.reshape(shared_by, cont_size, HD))
        gkv = jnp.concatenate([gk, gv], axis=1)
        cont_gkv.append(gkv[:span])
        own_gkv.append(gkv[span:])

    def kv_take(z_at, y_at):
        length = 2 * prompt_local
        def piece(values):
            return lax.dynamic_slice_in_dim(values, y_at * length, length, 0)

        total = jnp.where(z_at == z, piece(prompt_gkv), 0.0)
        for which, term in zip(which_prompt, cont_gkv):
            total = total + jnp.where(z_at == which, piece(term), 0.0)
        return total

    kv_sum = scatter_grid(kv_take).reshape(2, prompt_local, 2 * HD)
    halves = []
    for half in range(2):
        halves.append(kv_sum[half])
        halves.extend(own_gkv[half * cont_count : (half + 1) * cont_count])
    grad_kv = jnp.concatenate(halves, axis=0)
    grad_q = rows_order(prompt_gq.reshape(shared_by, 2, prompt_local, HD), cont_gq)
    grad_proj = jnp.concatenate(
        [
            rotary(grad_q[:, i * HD : (i + 1) * HD] * query_scale, cosine, -sine_wave)
            for i in range(shared_by)
        ]
        + [rotary(grad_kv[:, :HD], cosine, -sine_wave), grad_kv[:, HD:]],
        axis=1,
    ).astype(bf16)
    grad_attn_w = matmul_lt(chip_rows, grad_proj).astype(bf16)
    attn_sum = scatter_grid(taker(grad_attn_w.reshape(z_size, y_size, 2 * part, a_cols)))
    grad_one = to_shares(matmul_rt(grad_proj, attn_w))
    grad_input = grad_middle + norm_back(grad_one, take_share(normal_one), take_share(inverse_one))
    input_low = grad_input.astype(bf16)
    input_rows = rows_of(input_low, tp_swap(input_low)).astype(f32)

    def split_core(summed):
        mine = lax.dynamic_slice_in_dim(summed, core * part, part, 0)
        give = lax.dynamic_slice_in_dim(summed, (1 - core) * part, part, 0).astype(bf16)
        return mine, core_swap(give).astype(f32)

    out_mine, out_got = split_core(out_sum)
    first, second = by_core(out_mine[:, :q_cols], out_got[:, :q_cols])
    grad_out = jnp.concatenate([first, second], axis=1).T
    post_sum = out_mine[:, q_cols : q_cols + 2] + out_got[:, q_cols : q_cols + 2]
    attn_mine, attn_got = split_core(attn_sum)
    first, second = by_core(attn_mine, attn_got)

    def both_cores(start, size):
        return jnp.concatenate([first[:, start : start + size], second[:, start : start + size]], axis=1)

    raw_q = both_cores(0, q_cols)
    raw_k = both_cores(q_cols, kv_cols)
    raw_v = both_cores(q_cols + kv_cols, kv_cols)

    def gain_sum(raw, weight):
        return jnp.sum(raw * weight.astype(f32), axis=1)

    gain_terms = jnp.stack(
        [
            gain_sum(raw_q, w_query) + gain_sum(raw_k, w_key) + gain_sum(raw_v, w_value),
            post_sum[:, 0],
            gain_sum(raw_gate, w_gate) + gain_sum(raw_up, w_up),
            post_sum[:, 1],
        ],
        axis=0,
    )
    gain_grads = gain_terms + tp_swap(gain_terms)

    return (
        result_rows[:prompt_local].reshape(1, prompt_local, width),
        result_rows[prompt_local:].reshape(cont_count, cont_size, width),
        input_rows[:prompt_local].reshape(1, prompt_local, width),
        input_rows[prompt_local:].reshape(cont_count, cont_size, width),
        gain_grads[0],
        gain_grads[1],
        gain_grads[2],
        gain_grads[3],
        raw_q * gain_one,
        raw_k * gain_one,
        raw_v * gain_one,
        grad_out,
        raw_gate * gain_three,
        raw_up * gain_three,
        raw_down.T,
    )


def solution(mesh):
    in_specs = (
        P("fsdp", "ctx", None),
        P(("fsdp", "ctx"), None, None),
        P(("fsdp", "ctx")),
        P(("fsdp", "ctx")),
        P(("fsdp", "ctx")),
        P(("fsdp", "ctx")),
        P(("fsdp", "ctx")),
        P(("fsdp", "ctx")),
        P(("fsdp", "ctx"), "tp"),
        P(("fsdp", "ctx"), "tp"),
        P(("fsdp", "ctx"), "tp"),
        P("tp", ("fsdp", "ctx")),
        P(("fsdp", "ctx"), "tp"),
        P(("fsdp", "ctx"), "tp"),
        P("tp", ("fsdp", "ctx")),
        P("fsdp", "ctx", None),
        P(("fsdp", "ctx"), None, None),
    )
    out_specs = (
        P("fsdp", "ctx", None),
        P(("fsdp", "ctx"), None, None),
        P("fsdp", "ctx", None),
        P(("fsdp", "ctx"), None, None),
        P(("fsdp", "ctx")),
        P(("fsdp", "ctx")),
        P(("fsdp", "ctx")),
        P(("fsdp", "ctx")),
        P(("fsdp", "ctx"), "tp"),
        P(("fsdp", "ctx"), "tp"),
        P(("fsdp", "ctx"), "tp"),
        P("tp", ("fsdp", "ctx")),
        P(("fsdp", "ctx"), "tp"),
        P(("fsdp", "ctx"), "tp"),
        P("tp", ("fsdp", "ctx")),
    )
    return jax.shard_map(shards, mesh=mesh, in_specs=in_specs, out_specs=out_specs, check_vma=False)
```

```python
import math

import jax
import jax.numpy as jnp
from jax import lax
from jax.sharding import PartitionSpec as P

HD = 256
PROMPT = 1024

soft_cap = 50.0
norm_eps = 1e-06
masked_fill = -1e30
bf16 = jnp.bfloat16
f32 = jnp.float32


def norm_parts(values):
    inverse = lax.rsqrt(jnp.mean(values * values, axis=-1, keepdims=True) + norm_eps)
    return (values * inverse, inverse)


def norm_back(grad_normal, normal, inverse):
    return inverse * (
        grad_normal - normal * jnp.mean(grad_normal * normal, axis=-1, keepdims=True)
    )


def rotary_tables(places, head_dim):
    half_dim = head_dim // 2
    frequency = jnp.exp(
        jnp.arange(half_dim, dtype=f32) * (-2.0 * math.log(10000.0) / head_dim)
    )
    angles = places[:, None] * frequency[None, :]
    return (jnp.cos(angles), jnp.sin(angles))


def rotary(values, cosine, sine_wave):
    half_dim = values.shape[-1] // 2
    front_half = values[..., :half_dim]
    back_half = values[..., half_dim:]
    return jnp.concatenate(
        [front_half * cosine - back_half * sine_wave, back_half * cosine + front_half * sine_wave],
        axis=-1,
    )


def tie(first, *others):
    return lax.optimization_barrier((first,) + others)[0]


def matmul(left, right):
    return jnp.dot(left, right, preferred_element_type=f32)


def matmul_rt(left, right):
    return lax.dot_general(left, right, (((1,), (1,)), ((), ())), preferred_element_type=f32)


def matmul_lt(left, right):
    return lax.dot_general(left, right, (((0,), (0,)), ((), ())), preferred_element_type=f32)


def attend_forward(query, key, value, allowed):
    raw_scores = matmul_rt(query, key)
    capped = jnp.where(allowed, soft_cap * jnp.tanh(raw_scores / soft_cap), masked_fill)
    row_peak = jnp.max(capped, axis=-1, keepdims=True)
    exponent = jnp.exp(capped - row_peak)
    row_total = jnp.sum(exponent, axis=-1, keepdims=True)
    weight_set = (exponent / row_total).astype(bf16)
    return (matmul(weight_set, value), row_peak + jnp.log(row_total))


def attend_backward(query, key, value, allowed, log_total, grad_mixed):
    raw_scores = matmul_rt(query, key)
    squashed = jnp.tanh(raw_scores / soft_cap)
    capped = jnp.where(allowed, soft_cap * squashed, masked_fill)
    probabilities = jnp.exp(capped - log_total)
    weight_set = probabilities.astype(bf16)
    grad_value = matmul_lt(weight_set, grad_mixed)
    grad_probs = matmul_rt(grad_mixed, value)
    inner_sum = jnp.sum(probabilities * grad_probs, axis=-1, keepdims=True)
    grad_scores = (probabilities * (grad_probs - inner_sum) * (1.0 - squashed * squashed)).astype(
        bf16
    )
    return (matmul(grad_scores, key), matmul_lt(grad_scores, query), grad_value)


def shards(
    prompt_x,
    cont_x,
    cont_prompt,
    cont_len,
    attn_norm,
    attn_post,
    mlp_norm,
    mlp_post,
    w_query,
    w_key,
    w_value,
    w_out,
    w_gate,
    w_up,
    w_down,
    prompt_cot,
    cont_cot,
):
    width = prompt_x.shape[2]
    prompt_local = prompt_x.shape[1]
    cont_count = cont_x.shape[0]
    cont_size = cont_x.shape[1]
    cont_rows = cont_count * cont_size
    rows = prompt_local + cont_rows
    z_size = lax.axis_size("fsdp")
    c_size = lax.axis_size("ctx")
    y_size = c_size // 2
    z = lax.axis_index("fsdp")
    c = lax.axis_index("ctx")
    y = c // 2
    core = c % 2
    t = lax.axis_index("tp")
    part = w_query.shape[0]
    q_cols = w_query.shape[1] // 2
    kv_cols = w_key.shape[1] // 2
    shared_by = q_cols // kv_cols
    a_cols = q_cols + 2 * kv_cols
    block = w_gate.shape[1] // z_size
    share = rows // 2
    query_scale = HD ** (-0.5)

    def z_shift(values, step):
        return lax.ppermute(values, "fsdp", [(i, (i + step) % z_size) for i in range(z_size)])

    def y_next(values):
        return lax.ppermute(values, "ctx", [(i, (i + 2) % c_size) for i in range(c_size)])

    def core_swap(values):
        return lax.ppermute(values, "ctx", [(i, i ^ 1) for i in range(c_size)])

    def tp_swap(values):
        return lax.ppermute(values, "tp", [(0, 1), (1, 0)])

    def by_core(own, other):
        return (jnp.where(core == 0, own, other), jnp.where(core == 0, other, own))

    def place(held, piece, *index):
        piece = piece.reshape((1,) * len(index) + piece.shape)
        return lax.dynamic_update_slice(held, piece, index + (0,) * (held.ndim - len(index)))

    def gather_grid(own, waits=()):
        held = jnp.zeros((z_size, y_size) + own.shape, own.dtype)
        chunk, arrivals, extra = own, [], list(waits)
        for step in range(z_size):
            if step:
                chunk = tie(ahead, turn)
            ahead = z_shift(chunk, 1) if step < z_size - 1 else None
            if ahead is not None:
                arrivals.append(ahead)
            elif step:
                arrivals[-1] = chunk
            turn = chunk
            for hop in range(y_size):
                if hop:
                    turn = y_next(turn)
                held = place(held, turn, (z - step) % z_size, (y - hop) % y_size)
        return held, arrivals, None

    def row_of(values, at):
        return lax.dynamic_slice_in_dim(values, at, 1, 0)[0]

    def scatter_y(values):
        def column(at):
            return lax.dynamic_slice_in_dim(values, at, 1, 1)[:, 0].astype(f32)

        total = column((y - 1) % y_size)
        for hop in range(2, y_size + 1):
            total = y_next(total.astype(bf16)).astype(f32) + column((y - hop) % y_size)
        return total

    def scatter_z(values):
        low = values.astype(bf16)
        terms = [row_of(values, z)]
        for step in range(1, z_size):
            terms.append(z_shift(row_of(low, (z + step) % z_size), step))
        return terms

    def add_up(terms):
        total = terms[0].astype(f32)
        for term in terms[1:]:
            total = total + term.astype(f32)
        return total

    def scatter_grid(take, groups, waits=()):
        steps, sent = list(range(1, z_size)) + [0], {}
        for size in groups:
            now, steps = steps[:size], steps[size:]

            def terms(y_at):
                return jnp.stack([take((z + step) % z_size, y_at) for step in now], axis=0)

            total = terms((y - 1) % y_size)
            for hop in range(2, y_size + 1):
                total = y_next(total.astype(bf16)).astype(f32) + terms((y - hop) % y_size)
            if waits:
                total, waits = tie(total, waits[0]), waits[1:]
            for i, step in enumerate(now):
                sent[step] = z_shift(total[i].astype(bf16), step) if step else total[i]
        return [sent[step] for step in range(z_size)], total

    def taker(values):
        tail = (0,) * (values.ndim - 2)

        def take(z_at, y_at):
            piece = lax.dynamic_slice(values, (z_at, y_at) + tail, (1, 1) + values.shape[2:])
            return piece[0, 0].astype(f32)

        return take

    def take_share(values):
        return lax.dynamic_slice_in_dim(values, t * share, share, 0)

    def give_share(values):
        return lax.dynamic_slice_in_dim(values, (1 - t) * share, share, 0)

    def rows_of(mine, other):
        return jnp.concatenate(
            [jnp.where(t == 0, mine, other), jnp.where(t == 0, other, mine)], axis=0
        )

    gain_one = attn_norm.astype(f32)[:, None]
    gain_three = mlp_norm.astype(f32)[:, None]
    pairs = (2,) * (z_size // 2)
    same_core = [[y_at * 2 * 2 + which * 2 + t_at for y_at in range(y_size) for t_at in range(2)] for which in range(2)]

    def over_z(values):
        return lax.all_to_all(values, "fsdp", 0, 0, tiled=True)

    def z_blocks(local):
        return jnp.stack([local[:, i * block : (i + 1) * block] for i in range(z_size)], axis=0)

    scaled_q = (w_query.astype(f32) * gain_one).astype(bf16)
    scaled_k = (w_key.astype(f32) * gain_one).astype(bf16)
    scaled_v = (w_value.astype(f32) * gain_one).astype(bf16)

    gains = jnp.concatenate(
        [attn_post[:, None], mlp_post[:, None], jnp.zeros((part, 126), bf16)], axis=1
    )

    def head_cols(which):
        return jnp.concatenate(
            [
                lax.dynamic_slice_in_dim(scaled_q, which * q_cols, q_cols, 1),
                lax.dynamic_slice_in_dim(scaled_k, which * kv_cols, kv_cols, 1),
                lax.dynamic_slice_in_dim(scaled_v, which * kv_cols, kv_cols, 1),
                lax.dynamic_slice_in_dim(w_out.T, which * q_cols, q_cols, 1),
                gains,
            ],
            axis=1,
        )

    mine, other = by_core(head_cols(core), core_swap(head_cols(1 - core)))
    attn_own = jnp.stack([mine, other], axis=0)
    gate_low = z_blocks((w_gate.astype(f32) * gain_three).astype(bf16))
    up_low = z_blocks((w_up.astype(f32) * gain_three).astype(bf16))
    down_low = z_blocks(w_down.T)
    attn_grid, attn_z, _ = gather_grid(attn_own)
    gate_held = over_z(tie(gate_low, attn_z[-1]))
    attn_grid = attn_grid.reshape(width, a_cols + q_cols + 128)
    attn_w = attn_grid[:, :a_cols]
    out_w = attn_grid[:, a_cols : a_cols + q_cols]
    prompt_x, cont_x = tie((prompt_x, cont_x), attn_own)

    def spread(held):
        return lax.all_gather(
            held, ("ctx", "tp"), axis=0, tiled=False, axis_index_groups=same_core
        ).reshape((y_size, 2) + held.shape)

    def spread_end(every):
        mine = lax.dynamic_slice_in_dim(every, core, 1, 1)[:, 0]
        got = core_swap(lax.dynamic_slice_in_dim(every, 1 - core, 1, 1)[:, 0])
        full = jnp.zeros((z_size, y_size, 2, part, block), bf16)
        for which, rows_at in ((core, mine), (1 - core, got)):
            full = lax.dynamic_update_slice(
                full, rows_at.transpose(1, 0, 2, 3)[:, :, None], (0, 0, which, 0, 0)
            )
        return full.reshape(width, block)

    gate_every = spread(gate_held)
    up_held = over_z(tie(up_low, gate_held))
    up_every = spread(up_held)

    residual = jnp.concatenate(
        [prompt_x.reshape(prompt_local, width), cont_x.reshape(cont_rows, width)], axis=0
    ).astype(f32)
    normal_one, inverse_one = norm_parts(residual)
    normal_low = normal_one.astype(bf16)
    chip_rows = jnp.concatenate([normal_low, core_swap(normal_low)], axis=0)

    core_of = (core, 1 - core)
    cont_places = PROMPT + jnp.tile(jnp.arange(cont_size, dtype=jnp.int32), cont_count)
    prompt_places = [
        (y * 2 + which) * prompt_local + jnp.arange(prompt_local, dtype=jnp.int32)
        for which in core_of
    ]
    places = jnp.concatenate(
        [prompt_places[0], cont_places, prompt_places[1], cont_places]
    ).astype(f32)
    cosine, sine_wave = rotary_tables(places, HD)
    projected = matmul(chip_rows, attn_w)
    query_rows = jnp.stack(
        [
            (rotary(projected[:, i * HD : (i + 1) * HD], cosine, sine_wave) * query_scale).astype(bf16)
            for i in range(shared_by)
        ],
        axis=0,
    ).reshape(shared_by, 2, rows, HD)
    key_rows = rotary(projected[:, q_cols : q_cols + HD], cosine, sine_wave).astype(bf16)
    value_rows = projected[:, q_cols + HD :].astype(bf16)
    kv_rows = jnp.concatenate([key_rows, value_rows], axis=1).reshape(2, rows, 2 * HD)
    prompt_kv = kv_rows[:, :prompt_local].reshape(2 * prompt_local, 2 * HD)
    every_kv, kv_z, kv_y = gather_grid(tie(prompt_kv, up_held))
    every_kv = every_kv.reshape(z_size, y_size * 2 * prompt_local, 2 * HD)
    span = every_kv.shape[1]
    down_held = over_z(tie(down_low, kv_z[-1]))
    down_every = spread(down_held)
    every_kv = tie(every_kv, down_held)
    own_kv = lax.dynamic_slice(every_kv, (z, 0, 0), (1, span, 2 * HD))[0]
    key_places = (
        (jnp.arange(y_size, dtype=jnp.int32)[:, None, None] * 2
         + jnp.stack(core_of)[None, :, None]) * prompt_local
        + jnp.arange(prompt_local, dtype=jnp.int32)[None, None, :]
    ).reshape(1, span)
    head_places = jnp.tile(jnp.concatenate(prompt_places), shared_by)
    prompt_allowed = key_places <= head_places[:, None]
    cont_allowed = jnp.tile(
        jnp.arange(span + cont_size, dtype=jnp.int32)[None, :]
        <= span + jnp.arange(cont_size, dtype=jnp.int32)[:, None],
        (shared_by, 1),
    )
    prompt_query = query_rows[:, :, :prompt_local].reshape(-1, HD)
    prompt_mixed, prompt_total = attend_forward(
        prompt_query, own_kv[:, :HD], own_kv[:, HD:], prompt_allowed
    )
    prompt_mixed = prompt_mixed.astype(bf16).reshape(shared_by, 2, prompt_local, HD)
    other_prompt = core_swap(cont_prompt)
    which_prompt = [cont_prompt[i] for i in range(cont_count)] + [
        other_prompt[i] for i in range(cont_count)
    ]
    conts = []
    for i in range(2 * cont_count):
        at = prompt_local + (i % cont_count) * cont_size
        half = i // cont_count
        kv = jnp.concatenate(
            [
                lax.dynamic_slice(every_kv, (which_prompt[i], 0, 0), (1, span, 2 * HD))[0],
                kv_rows[half, at : at + cont_size],
            ],
            axis=0,
        )
        query = query_rows[:, half, at : at + cont_size].reshape(-1, HD)
        mixed, total = attend_forward(query, kv[:, :HD], kv[:, HD:], cont_allowed)
        conts.append((query, kv, mixed.astype(bf16).reshape(shared_by, cont_size, HD), total))

    def rows_order(prompt_part, cont_parts):
        halves = []
        for half in range(2):
            pieces = [prompt_part[:, half]] + cont_parts[half * cont_count : (half + 1) * cont_count]
            halves.append(jnp.concatenate(pieces, axis=1))
        heads = jnp.concatenate(halves, axis=1)
        return jnp.concatenate([heads[i] for i in range(shared_by)], axis=1)

    attn_out = rows_order(prompt_mixed, [entry[2] for entry in conts])

    def to_shares(partial):
        low = partial.astype(bf16)
        summed = partial[:rows] + core_swap(low[rows:]).astype(f32)
        return take_share(summed) + tp_swap(give_share(summed).astype(bf16)).astype(f32)

    pick = (
        jnp.arange(8, dtype=jnp.int32)[:, None] == jnp.arange(128, dtype=jnp.int32)[None, :]
    ).astype(bf16)
    post_rows = matmul_rt(pick, attn_grid[:, a_cols + q_cols :])
    post_attn, post_mlp = post_rows[0:1], post_rows[1:2]
    branch_partial = matmul_rt(attn_out, out_w)
    branch_core = branch_partial[:rows] + core_swap(branch_partial[rows:].astype(bf16)).astype(f32)
    branch_give = give_share(branch_core).astype(bf16)
    branch_got = tp_swap(branch_give)
    gate_w = spread_end(tie(gate_every, branch_give))
    branch = take_share(branch_core) + tie(branch_got, gate_w).astype(f32)
    up_w = spread_end(up_every)

    normal_two, inverse_two = norm_parts(branch)
    middle = take_share(residual) + normal_two * post_attn
    normal_three, inverse_three = norm_parts(middle)

    three_low = normal_three.astype(bf16)
    down_w = spread_end(tie(down_every, three_low))

    def ring_rows(own, step_fn, before_last=None, own_first=False):
        sums = []
        chunk = own
        for step in range(z_size):
            if step:
                chunk = z_shift(chunk, 1)
            if step == 1 and own_first:
                chunk = tie(chunk, partial)
            both = jnp.concatenate([chunk, core_swap(chunk)], axis=0)
            partial = step_fn(step, both)
            sums.append(
                partial[:share] + core_swap(partial[share:].astype(bf16)).astype(f32)
            )
        total, lows = sums[1], []
        for step in list(range(2, z_size)) + [0]:
            lows.append(total.astype(bf16))
            if step == 0 and before_last is not None:
                lows[-1] = tie(lows[-1], before_last())
            total = z_shift(lows[-1], 1).astype(f32) + sums[step]
        return total, lows

    mlp_in, gates, ups, inners = {}, {}, {}, {}

    def mlp_forward(step, both):
        mlp_in[step] = both
        gates[step] = matmul(both, gate_w)
        ups[step] = matmul(both, up_w)
        inners[step] = (jax.nn.gelu(gates[step], approximate=True) * ups[step]).astype(bf16)
        return matmul_rt(inners[step], down_w)

    mlp_share, _ = ring_rows(three_low, mlp_forward)

    normal_four, inverse_four = norm_parts(mlp_share)
    cont_live = (
        (jnp.arange(cont_size, dtype=jnp.int32)[None, :] < cont_len[:, None])
        .astype(f32)
        .reshape(cont_rows)
    )
    live_rows = jnp.concatenate([jnp.ones((prompt_local,), f32), cont_live])
    live = take_share(live_rows)[:, None]
    result_share = ((middle + normal_four * post_mlp) * live).astype(bf16)
    result_rows = rows_of(result_share, tp_swap(result_share))
    cot_rows = jnp.concatenate(
        [prompt_cot.reshape(prompt_local, width), cont_cot.reshape(cont_rows, width)], axis=0
    )
    grad_result = take_share(cot_rows).astype(f32) * live
    grad_post_mlp = jnp.sum(grad_result * normal_four, axis=0)
    grad_mlp = norm_back(grad_result * post_mlp, normal_four, inverse_four)

    grad_outs, grad_gates, grad_ups = {}, {}, {}

    def mlp_backward(step, both):
        grad_outs[step] = both
        grad_inner = matmul(both, down_w)
        pull = jax.vjp(
            lambda gate_in, up_in: jax.nn.gelu(gate_in, approximate=True) * up_in,
            gates[step],
            ups[step],
        )[1]
        grad_gate, grad_up = pull(grad_inner)
        grad_gates[step] = grad_gate.astype(bf16)
        grad_ups[step] = grad_up.astype(bf16)
        return matmul_rt(grad_gates[step], gate_w) + matmul_rt(grad_ups[step], up_w)

    def blocks_back(got):
        return jnp.concatenate([got[i] for i in range(z_size)], axis=1).astype(f32)

    def reduce_terms(full):
        full = full.reshape(z_size, y_size, 2, part, block)

        def of_core(which):
            return lax.dynamic_slice_in_dim(full, which, 1, 2)[:, :, 0].transpose(1, 0, 2, 3)

        halves = by_core(of_core(core), core_swap(of_core(1 - core)))
        return jnp.stack(halves, axis=1).reshape((y_size * 2 * z_size,) + full.shape[3:])

    def reduce(every):
        return lax.psum_scatter(
            every, ("ctx", "tp"), scatter_dimension=0, tiled=True, axis_index_groups=same_core
        )

    def joined(pieces):
        return jnp.concatenate([pieces[step] for step in range(z_size)], axis=0)

    down_terms = []

    def before_last():
        grad_down_w = matmul_lt(joined(grad_outs), joined(inners)).astype(bf16)
        down_terms.append(reduce_terms(grad_down_w))
        return down_terms[0]

    grad_three, lows = ring_rows(grad_mlp.astype(bf16), mlp_backward, before_last, True)
    down_sum = reduce(down_terms[0])
    all_in = joined(mlp_in)
    grad_gate_w = matmul_lt(tie(all_in, lows[2]), joined(grad_gates)).astype(bf16)
    gate_terms = reduce_terms(grad_gate_w)
    gate_sum = reduce(gate_terms)
    grad_three = tie(grad_three, gate_terms)

    grad_middle = grad_result + norm_back(grad_three, normal_three, inverse_three)
    grad_post_attn = jnp.sum(grad_middle * normal_two, axis=0)
    grad_branch = norm_back(grad_middle * post_attn, normal_two, inverse_two).astype(bf16)
    grad_up_w = matmul_lt(tie(all_in, grad_branch), joined(grad_ups)).astype(bf16)
    up_terms = reduce_terms(grad_up_w)
    up_sum = reduce(up_terms)
    down_got = over_z(tie(down_sum, grad_branch))
    branch_rows = rows_of(grad_branch, tie(tp_swap(grad_branch), up_terms, down_got))
    branch_chip = jnp.concatenate([branch_rows, core_swap(branch_rows)], axis=0)
    grad_attn = matmul(branch_chip, out_w).astype(bf16)
    grad_out_w = matmul_lt(tie(branch_chip, grad_attn), attn_out).astype(bf16)
    out_y = scatter_y(grad_out_w.reshape(z_size, y_size, 2 * part, q_cols)).astype(bf16)
    grad_heads = jnp.stack(
        [grad_attn[:, i * HD : (i + 1) * HD] for i in range(shared_by)], axis=0
    ).reshape(shared_by, 2, rows, HD)
    prompt_gq, prompt_gk, prompt_gv = attend_backward(
        prompt_query,
        own_kv[:, :HD],
        own_kv[:, HD:],
        prompt_allowed,
        prompt_total,
        grad_heads[:, :, :prompt_local].reshape(-1, HD),
    )
    prompt_gkv = jnp.concatenate([prompt_gk, prompt_gv], axis=1)
    gate_got = over_z(tie(gate_sum, grad_attn))
    grad_heads = tie(grad_heads, gate_got)
    cont_gq, cont_gkv, own_gkv = [], [], []
    for i in range(2 * cont_count):
        at = prompt_local + (i % cont_count) * cont_size
        half = i // cont_count
        query, kv, _, total = conts[i]
        gq, gk, gv = attend_backward(
            query,
            kv[:, :HD],
            kv[:, HD:],
            cont_allowed,
            total,
            grad_heads[:, half, at : at + cont_size].reshape(-1, HD),
        )
        cont_gq.append(gq.reshape(shared_by, cont_size, HD))
        gkv = jnp.concatenate([gk, gv], axis=1)
        cont_gkv.append(gkv[:span])
        own_gkv.append(gkv[span:])

    def kv_take(z_at, y_at):
        length = 2 * prompt_local

        def piece(values):
            return lax.dynamic_slice_in_dim(values, y_at * length, length, 0)

        total = jnp.where(z_at == z, piece(prompt_gkv), 0.0)
        for which, term in zip(which_prompt, cont_gkv):
            total = total + jnp.where(z_at == which, piece(term), 0.0)
        return total

    out_got = over_z(out_y)
    kv_terms, kv_total = scatter_grid(kv_take, pairs, (out_y, out_got))
    grad_q = rows_order(prompt_gq.reshape(shared_by, 2, prompt_local, HD), cont_gq)
    grad_q_proj = jnp.concatenate(
        [
            rotary(grad_q[:, i * HD : (i + 1) * HD] * query_scale, cosine, -sine_wave)
            for i in range(shared_by)
        ],
        axis=1,
    ).astype(bf16)
    grad_q_w = matmul_lt(chip_rows, grad_q_proj).astype(bf16)
    post_terms = jnp.stack([grad_post_attn, grad_post_mlp], axis=0)
    post_terms = post_terms.reshape(2, z_size, y_size, 2, part).transpose(1, 2, 3, 0, 4)
    q_y = scatter_y(tie(grad_q_w, kv_total).reshape(z_size, y_size, 2 * part, q_cols))
    kv_low = add_up(tie(kv_terms, q_y))
    up_got = over_z(tie(up_sum, q_y))
    kv_sum = kv_low.reshape(2, prompt_local, 2 * HD)
    halves = []
    for half in range(2):
        halves.append(kv_sum[half])
        halves.extend(own_gkv[half * cont_count : (half + 1) * cont_count])
    grad_kv = jnp.concatenate(halves, axis=0)
    grad_kv_proj = jnp.concatenate(
        [rotary(grad_kv[:, :HD], cosine, -sine_wave), grad_kv[:, HD:]], axis=1
    ).astype(bf16)
    one_partial = matmul_rt(grad_q_proj, attn_w[:, :q_cols]) + matmul_rt(
        grad_kv_proj, attn_w[:, q_cols:]
    )
    one_core = one_partial[:rows] + core_swap(one_partial[rows:].astype(bf16)).astype(f32)
    one_give = give_share(one_core).astype(bf16)
    one_got = tp_swap(one_give)
    grad_kv_w = matmul_lt(tie(chip_rows, one_give), grad_kv_proj).astype(bf16)
    kvw_y = scatter_y(grad_kv_w.reshape(z_size, y_size, 2 * part, 2 * kv_cols))
    q_got = over_z(tie(q_y, up_got).astype(bf16))
    one_got = tie(one_got, up_got, q_got, kvw_y)
    grad_one = take_share(one_core) + one_got.astype(f32)
    post_z = scatter_z(scatter_y(tie(post_terms, one_give)))
    grad_input = grad_middle + norm_back(grad_one, take_share(normal_one), take_share(inverse_one))
    input_low = grad_input.astype(bf16)
    kvw_got = over_z(kvw_y.astype(bf16))
    raw_down = blocks_back(tie(down_got, input_low))
    raw_gate = blocks_back(tie(gate_got, input_low))
    raw_up = blocks_back(tie(up_got, input_low))
    out_sum = jnp.sum(tie(out_got, input_low).astype(f32), axis=0)
    q_sum = jnp.sum(tie(q_got, input_low).astype(f32), axis=0)
    kvw_sum = jnp.sum(tie(kvw_got, input_low).astype(f32), axis=0)
    post_sum = add_up(tie(post_z, input_low))
    input_rows = rows_of(input_low, tp_swap(input_low)).astype(f32)

    def split_core(summed):
        mine = lax.dynamic_slice_in_dim(summed, core * part, part, 0)
        give = lax.dynamic_slice_in_dim(summed, (1 - core) * part, part, 0).astype(bf16)
        return mine, core_swap(give).astype(f32)

    grad_out = jnp.concatenate(by_core(*split_core(out_sum)), axis=1).T
    post_sum = row_of(post_sum, core) + core_swap(row_of(post_sum, 1 - core))
    raw_q = jnp.concatenate(by_core(*split_core(q_sum)), axis=1)
    first, second = by_core(*split_core(kvw_sum))
    raw_k = jnp.concatenate([first[:, :kv_cols], second[:, :kv_cols]], axis=1)
    raw_v = jnp.concatenate([first[:, kv_cols:], second[:, kv_cols:]], axis=1)

    def gain_sum(raw, weight):
        return jnp.sum(raw * weight.astype(f32), axis=1)

    gain_terms = jnp.stack(
        [
            gain_sum(raw_q, w_query) + gain_sum(raw_k, w_key) + gain_sum(raw_v, w_value),
            post_sum[0],
            gain_sum(raw_gate, w_gate) + gain_sum(raw_up, w_up),
            post_sum[1],
        ],
        axis=0,
    )
    gain_grads = gain_terms + tp_swap(gain_terms)

    return (
        result_rows[:prompt_local].reshape(1, prompt_local, width),
        result_rows[prompt_local:].reshape(cont_count, cont_size, width),
        input_rows[:prompt_local].reshape(1, prompt_local, width),
        input_rows[prompt_local:].reshape(cont_count, cont_size, width),
        gain_grads[0],
        gain_grads[1],
        gain_grads[2],
        gain_grads[3],
        raw_q * gain_one,
        raw_k * gain_one,
        raw_v * gain_one,
        grad_out,
        raw_gate * gain_three,
        raw_up * gain_three,
        raw_down.T,
    )


def solution(mesh):
    in_specs = (
        P("fsdp", "ctx", None),
        P(("fsdp", "ctx"), None, None),
        P(("fsdp", "ctx")),
        P(("fsdp", "ctx")),
        P(("fsdp", "ctx")),
        P(("fsdp", "ctx")),
        P(("fsdp", "ctx")),
        P(("fsdp", "ctx")),
        P(("fsdp", "ctx"), "tp"),
        P(("fsdp", "ctx"), "tp"),
        P(("fsdp", "ctx"), "tp"),
        P("tp", ("fsdp", "ctx")),
        P(("fsdp", "ctx"), "tp"),
        P(("fsdp", "ctx"), "tp"),
        P("tp", ("fsdp", "ctx")),
        P("fsdp", "ctx", None),
        P(("fsdp", "ctx"), None, None),
    )
    out_specs = (
        P("fsdp", "ctx", None),
        P(("fsdp", "ctx"), None, None),
        P("fsdp", "ctx", None),
        P(("fsdp", "ctx"), None, None),
        P(("fsdp", "ctx")),
        P(("fsdp", "ctx")),
        P(("fsdp", "ctx")),
        P(("fsdp", "ctx")),
        P(("fsdp", "ctx"), "tp"),
        P(("fsdp", "ctx"), "tp"),
        P(("fsdp", "ctx"), "tp"),
        P("tp", ("fsdp", "ctx")),
        P(("fsdp", "ctx"), "tp"),
        P(("fsdp", "ctx"), "tp"),
        P("tp", ("fsdp", "ctx")),
    )
    return jax.shard_map(shards, mesh=mesh, in_specs=in_specs, out_specs=out_specs, check_vma=False)
```

```python
import math

import jax
import jax.numpy as jnp
from jax import lax
from jax.sharding import PartitionSpec as P

HD = 256
PROMPT = 1024

soft_cap = 50.0
norm_eps = 1e-06
masked_fill = -1e30
bf16 = jnp.bfloat16
f32 = jnp.float32


def norm_parts(values):
    inverse = lax.rsqrt(jnp.mean(values * values, axis=-1, keepdims=True) + norm_eps)
    return (values * inverse, inverse)


def norm_back(grad_normal, normal, inverse):
    return inverse * (
        grad_normal - normal * jnp.mean(grad_normal * normal, axis=-1, keepdims=True)
    )


def rotary_tables(places, head_dim):
    half_dim = head_dim // 2
    frequency = jnp.exp(
        jnp.arange(half_dim, dtype=f32) * (-2.0 * math.log(10000.0) / head_dim)
    )
    angles = places[:, None] * frequency[None, :]
    return (jnp.cos(angles), jnp.sin(angles))


def rotary(values, cosine, sine_wave):
    half_dim = values.shape[-1] // 2
    front_half = values[..., :half_dim]
    back_half = values[..., half_dim:]
    return jnp.concatenate(
        [front_half * cosine - back_half * sine_wave, back_half * cosine + front_half * sine_wave],
        axis=-1,
    )


def tie(first, *others):
    return lax.optimization_barrier((first,) + others)[0]


def matmul(left, right):
    return jnp.dot(left, right, preferred_element_type=f32)


def matmul_rt(left, right):
    return lax.dot_general(left, right, (((1,), (1,)), ((), ())), preferred_element_type=f32)


def matmul_lt(left, right):
    return lax.dot_general(left, right, (((0,), (0,)), ((), ())), preferred_element_type=f32)


def attend_forward(query, key, value, allowed):
    raw_scores = matmul_rt(query, key)
    capped = jnp.where(allowed, soft_cap * jnp.tanh(raw_scores / soft_cap), masked_fill)
    row_peak = jnp.max(capped, axis=-1, keepdims=True)
    exponent = jnp.exp(capped - row_peak)
    row_total = jnp.sum(exponent, axis=-1, keepdims=True)
    weight_set = (exponent / row_total).astype(bf16)
    return (matmul(weight_set, value), row_peak + jnp.log(row_total))


def attend_backward(query, key, value, allowed, log_total, grad_mixed):
    raw_scores = matmul_rt(query, key)
    squashed = jnp.tanh(raw_scores / soft_cap)
    capped = jnp.where(allowed, soft_cap * squashed, masked_fill)
    probabilities = jnp.exp(capped - log_total)
    weight_set = probabilities.astype(bf16)
    grad_value = matmul_lt(weight_set, grad_mixed)
    grad_probs = matmul_rt(grad_mixed, value)
    inner_sum = jnp.sum(probabilities * grad_probs, axis=-1, keepdims=True)
    grad_scores = (probabilities * (grad_probs - inner_sum) * (1.0 - squashed * squashed)).astype(
        bf16
    )
    return (matmul(grad_scores, key), matmul_lt(grad_scores, query), grad_value)


def shards(
    prompt_x,
    cont_x,
    cont_prompt,
    cont_len,
    attn_norm,
    attn_post,
    mlp_norm,
    mlp_post,
    w_query,
    w_key,
    w_value,
    w_out,
    w_gate,
    w_up,
    w_down,
    prompt_cot,
    cont_cot,
):
    width = prompt_x.shape[2]
    prompt_local = prompt_x.shape[1]
    cont_count = cont_x.shape[0]
    cont_size = cont_x.shape[1]
    cont_rows = cont_count * cont_size
    rows = prompt_local + cont_rows
    z_size = lax.axis_size("fsdp")
    c_size = lax.axis_size("ctx")
    y_size = c_size // 2
    z = lax.axis_index("fsdp")
    c = lax.axis_index("ctx")
    y = c // 2
    core = c % 2
    t = lax.axis_index("tp")
    part = w_query.shape[0]
    q_cols = w_query.shape[1] // 2
    kv_cols = w_key.shape[1] // 2
    shared_by = q_cols // kv_cols
    a_cols = q_cols + 2 * kv_cols
    block = w_gate.shape[1] // z_size
    share = rows // 2
    query_scale = HD ** (-0.5)

    def z_shift(values, step):
        return lax.ppermute(values, "fsdp", [(i, (i + step) % z_size) for i in range(z_size)])

    def y_next(values):
        return lax.ppermute(values, "ctx", [(i, (i + 2) % c_size) for i in range(c_size)])

    def core_swap(values):
        return lax.ppermute(values, "ctx", [(i, i ^ 1) for i in range(c_size)])

    def tp_swap(values):
        return lax.ppermute(values, "tp", [(0, 1), (1, 0)])

    def by_core(own, other):
        return (jnp.where(core == 0, own, other), jnp.where(core == 0, other, own))

    def place(held, piece, *index):
        piece = piece.reshape((1,) * len(index) + piece.shape)
        return lax.dynamic_update_slice(held, piece, index + (0,) * (held.ndim - len(index)))

    def gather_grid(own, waits=()):
        held = jnp.zeros((z_size, y_size) + own.shape, own.dtype)
        chunk, arrivals, extra = own, [], list(waits)
        for step in range(z_size):
            if step:
                chunk = tie(ahead, turn)
            ahead = z_shift(chunk, 1) if step < z_size - 1 else None
            if ahead is not None:
                arrivals.append(ahead)
            elif step:
                arrivals[-1] = chunk
            turn = chunk
            for hop in range(y_size):
                if hop:
                    turn = y_next(turn)
                held = place(held, turn, (z - step) % z_size, (y - hop) % y_size)
        return held, arrivals, None

    def row_of(values, at):
        return lax.dynamic_slice_in_dim(values, at, 1, 0)[0]

    def scatter_y(values):
        def column(at):
            return lax.dynamic_slice_in_dim(values, at, 1, 1)[:, 0].astype(f32)

        total = column((y - 1) % y_size)
        for hop in range(2, y_size + 1):
            total = y_next(total.astype(bf16)).astype(f32) + column((y - hop) % y_size)
        return total

    def scatter_z(values):
        low = values.astype(bf16)
        terms = [row_of(values, z)]
        for step in range(1, z_size):
            terms.append(z_shift(row_of(low, (z + step) % z_size), step))
        return terms

    def add_up(terms):
        total = terms[0].astype(f32)
        for term in terms[1:]:
            total = total + term.astype(f32)
        return total

    def scatter_grid(take, groups, waits=()):
        steps, sent = list(range(1, z_size)) + [0], {}
        for size in groups:
            now, steps = steps[:size], steps[size:]

            def terms(y_at):
                return jnp.stack([take((z + step) % z_size, y_at) for step in now], axis=0)

            total = terms((y - 1) % y_size)
            for hop in range(2, y_size + 1):
                total = y_next(total.astype(bf16)).astype(f32) + terms((y - hop) % y_size)
            if waits:
                total, waits = tie(total, waits[0]), waits[1:]
            for i, step in enumerate(now):
                sent[step] = z_shift(total[i].astype(bf16), step) if step else total[i]
        return [sent[step] for step in range(z_size)], total

    def taker(values):
        tail = (0,) * (values.ndim - 2)

        def take(z_at, y_at):
            piece = lax.dynamic_slice(values, (z_at, y_at) + tail, (1, 1) + values.shape[2:])
            return piece[0, 0].astype(f32)

        return take

    def take_share(values):
        return lax.dynamic_slice_in_dim(values, t * share, share, 0)

    def give_share(values):
        return lax.dynamic_slice_in_dim(values, (1 - t) * share, share, 0)

    def rows_of(mine, other):
        return jnp.concatenate(
            [jnp.where(t == 0, mine, other), jnp.where(t == 0, other, mine)], axis=0
        )

    gain_one = attn_norm.astype(f32)[:, None]
    gain_three = mlp_norm.astype(f32)[:, None]
    pairs = (2,) * (z_size // 2)
    same_core = [[y_at * 2 * 2 + which * 2 + t_at for y_at in range(y_size) for t_at in range(2)] for which in range(2)]

    def over_z(values):
        return lax.all_to_all(values, "fsdp", 0, 0, tiled=True)

    def z_blocks(local):
        return jnp.stack([local[:, i * block : (i + 1) * block] for i in range(z_size)], axis=0)

    scaled_q = (w_query.astype(f32) * gain_one).astype(bf16)
    scaled_k = (w_key.astype(f32) * gain_one).astype(bf16)
    scaled_v = (w_value.astype(f32) * gain_one).astype(bf16)

    gains = jnp.concatenate(
        [attn_post[:, None], mlp_post[:, None], jnp.zeros((part, 126), bf16)], axis=1
    )

    def head_cols(which):
        return jnp.concatenate(
            [
                lax.dynamic_slice_in_dim(scaled_q, which * q_cols, q_cols, 1),
                lax.dynamic_slice_in_dim(scaled_k, which * kv_cols, kv_cols, 1),
                lax.dynamic_slice_in_dim(scaled_v, which * kv_cols, kv_cols, 1),
                lax.dynamic_slice_in_dim(w_out.T, which * q_cols, q_cols, 1),
                gains,
            ],
            axis=1,
        )

    mine, other = by_core(head_cols(core), core_swap(head_cols(1 - core)))
    attn_own = jnp.stack([mine, other], axis=0)
    gate_low = z_blocks((w_gate.astype(f32) * gain_three).astype(bf16))
    up_low = z_blocks((w_up.astype(f32) * gain_three).astype(bf16))
    down_low = z_blocks(w_down.T)
    attn_grid, attn_z, _ = gather_grid(attn_own)
    gate_held = over_z(tie(gate_low, attn_z[-1]))
    attn_grid = attn_grid.reshape(width, a_cols + q_cols + 128)
    attn_w = attn_grid[:, :a_cols]
    out_w = attn_grid[:, a_cols : a_cols + q_cols]
    prompt_x, cont_x = tie((prompt_x, cont_x), attn_own)

    def spread(held):
        return lax.all_gather(
            held, ("ctx", "tp"), axis=0, tiled=False, axis_index_groups=same_core
        ).reshape((y_size, 2) + held.shape)

    def spread_end(every):
        mine = lax.dynamic_slice_in_dim(every, core, 1, 1)[:, 0]
        got = core_swap(lax.dynamic_slice_in_dim(every, 1 - core, 1, 1)[:, 0])
        full = jnp.zeros((z_size, y_size, 2, part, block), bf16)
        for which, rows_at in ((core, mine), (1 - core, got)):
            full = lax.dynamic_update_slice(
                full, rows_at.transpose(1, 0, 2, 3)[:, :, None], (0, 0, which, 0, 0)
            )
        return full.reshape(width, block)

    gate_every = spread(gate_held)
    up_held = over_z(tie(up_low, gate_held))
    up_every = spread(up_held)

    residual = jnp.concatenate(
        [prompt_x.reshape(prompt_local, width), cont_x.reshape(cont_rows, width)], axis=0
    ).astype(f32)
    normal_one, inverse_one = norm_parts(residual)
    normal_low = normal_one.astype(bf16)
    chip_rows = jnp.concatenate([normal_low, core_swap(normal_low)], axis=0)

    core_of = (core, 1 - core)
    cont_places = PROMPT + jnp.tile(jnp.arange(cont_size, dtype=jnp.int32), cont_count)
    prompt_places = [
        (y * 2 + which) * prompt_local + jnp.arange(prompt_local, dtype=jnp.int32)
        for which in core_of
    ]
    places = jnp.concatenate(
        [prompt_places[0], cont_places, prompt_places[1], cont_places]
    ).astype(f32)
    cosine, sine_wave = rotary_tables(places, HD)
    projected = matmul(chip_rows, attn_w)
    query_rows = jnp.stack(
        [
            (rotary(projected[:, i * HD : (i + 1) * HD], cosine, sine_wave) * query_scale).astype(bf16)
            for i in range(shared_by)
        ],
        axis=0,
    ).reshape(shared_by, 2, rows, HD)
    key_rows = rotary(projected[:, q_cols : q_cols + HD], cosine, sine_wave).astype(bf16)
    value_rows = projected[:, q_cols + HD :].astype(bf16)
    kv_rows = jnp.concatenate([key_rows, value_rows], axis=1).reshape(2, rows, 2 * HD)
    prompt_kv = kv_rows[:, :prompt_local].reshape(2 * prompt_local, 2 * HD)
    every_kv, kv_z, kv_y = gather_grid(tie(prompt_kv, up_held))
    every_kv = every_kv.reshape(z_size, y_size * 2 * prompt_local, 2 * HD)
    span = every_kv.shape[1]
    down_held = over_z(tie(down_low, kv_z[-1]))
    down_every = spread(down_held)
    every_kv = tie(every_kv, down_held)
    own_kv = lax.dynamic_slice(every_kv, (z, 0, 0), (1, span, 2 * HD))[0]
    key_places = (
        (jnp.arange(y_size, dtype=jnp.int32)[:, None, None] * 2
         + jnp.stack(core_of)[None, :, None]) * prompt_local
        + jnp.arange(prompt_local, dtype=jnp.int32)[None, None, :]
    ).reshape(1, span)
    head_places = jnp.tile(jnp.concatenate(prompt_places), shared_by)
    prompt_allowed = key_places <= head_places[:, None]
    cont_allowed = jnp.tile(
        jnp.arange(span + cont_size, dtype=jnp.int32)[None, :]
        <= span + jnp.arange(cont_size, dtype=jnp.int32)[:, None],
        (shared_by, 1),
    )
    prompt_query = query_rows[:, :, :prompt_local].reshape(-1, HD)
    prompt_mixed, prompt_total = attend_forward(
        prompt_query, own_kv[:, :HD], own_kv[:, HD:], prompt_allowed
    )
    prompt_mixed = prompt_mixed.astype(bf16).reshape(shared_by, 2, prompt_local, HD)
    other_prompt = core_swap(cont_prompt)
    which_prompt = [cont_prompt[i] for i in range(cont_count)] + [
        other_prompt[i] for i in range(cont_count)
    ]
    conts = []
    for i in range(2 * cont_count):
        at = prompt_local + (i % cont_count) * cont_size
        half = i // cont_count
        kv = jnp.concatenate(
            [
                lax.dynamic_slice(every_kv, (which_prompt[i], 0, 0), (1, span, 2 * HD))[0],
                kv_rows[half, at : at + cont_size],
            ],
            axis=0,
        )
        query = query_rows[:, half, at : at + cont_size].reshape(-1, HD)
        mixed, total = attend_forward(query, kv[:, :HD], kv[:, HD:], cont_allowed)
        conts.append((query, kv, mixed.astype(bf16).reshape(shared_by, cont_size, HD), total))

    def rows_order(prompt_part, cont_parts):
        halves = []
        for half in range(2):
            pieces = [prompt_part[:, half]] + cont_parts[half * cont_count : (half + 1) * cont_count]
            halves.append(jnp.concatenate(pieces, axis=1))
        heads = jnp.concatenate(halves, axis=1)
        return jnp.concatenate([heads[i] for i in range(shared_by)], axis=1)

    attn_out = rows_order(prompt_mixed, [entry[2] for entry in conts])

    def to_shares(partial):
        low = partial.astype(bf16)
        summed = partial[:rows] + core_swap(low[rows:]).astype(f32)
        return take_share(summed) + tp_swap(give_share(summed).astype(bf16)).astype(f32)

    pick = (
        jnp.arange(8, dtype=jnp.int32)[:, None] == jnp.arange(128, dtype=jnp.int32)[None, :]
    ).astype(bf16)
    post_rows = matmul_rt(pick, attn_grid[:, a_cols + q_cols :])
    post_attn, post_mlp = post_rows[0:1], post_rows[1:2]
    branch_partial = matmul_rt(attn_out, out_w)
    branch_core = branch_partial[:rows] + core_swap(branch_partial[rows:].astype(bf16)).astype(f32)
    branch_give = give_share(branch_core).astype(bf16)
    branch_got = tp_swap(branch_give)
    gate_w = spread_end(tie(gate_every, branch_give))
    branch = take_share(branch_core) + tie(branch_got, gate_w).astype(f32)
    up_w = spread_end(up_every)

    normal_two, inverse_two = norm_parts(branch)
    middle = take_share(residual) + normal_two * post_attn
    normal_three, inverse_three = norm_parts(middle)

    three_low = normal_three.astype(bf16)
    down_w = spread_end(tie(down_every, three_low))

    def ring_rows(own, step_fn, before_last=None, own_first=False):
        sums = []
        chunk = own
        for step in range(z_size):
            if step:
                chunk = z_shift(chunk, 1)
            if step == 1 and own_first:
                chunk = tie(chunk, partial)
            both = jnp.concatenate([chunk, core_swap(chunk)], axis=0)
            partial = step_fn(step, both)
            sums.append(
                partial[:share] + core_swap(partial[share:].astype(bf16)).astype(f32)
            )
        total, lows = sums[1], []
        for step in list(range(2, z_size)) + [0]:
            lows.append(total.astype(bf16))
            if step == 0 and before_last is not None:
                lows[-1] = tie(lows[-1], before_last())
            total = z_shift(lows[-1], 1).astype(f32) + sums[step]
        return total, lows

    mlp_in, gates, ups, inners = {}, {}, {}, {}

    def mlp_forward(step, both):
        mlp_in[step] = both
        gates[step] = matmul(both, gate_w)
        ups[step] = matmul(both, up_w)
        inners[step] = (jax.nn.gelu(gates[step], approximate=True) * ups[step]).astype(bf16)
        return matmul_rt(inners[step], down_w)

    mlp_share, _ = ring_rows(three_low, mlp_forward)

    normal_four, inverse_four = norm_parts(mlp_share)
    cont_live = (
        (jnp.arange(cont_size, dtype=jnp.int32)[None, :] < cont_len[:, None])
        .astype(f32)
        .reshape(cont_rows)
    )
    live_rows = jnp.concatenate([jnp.ones((prompt_local,), f32), cont_live])
    live = take_share(live_rows)[:, None]
    result_share = ((middle + normal_four * post_mlp) * live).astype(bf16)
    result_rows = rows_of(result_share, tp_swap(result_share))
    cot_rows = jnp.concatenate(
        [prompt_cot.reshape(prompt_local, width), cont_cot.reshape(cont_rows, width)], axis=0
    )
    grad_result = take_share(cot_rows).astype(f32) * live
    grad_post_mlp = jnp.sum(grad_result * normal_four, axis=0)
    grad_mlp = norm_back(grad_result * post_mlp, normal_four, inverse_four)

    grad_outs, grad_gates, grad_ups = {}, {}, {}

    def mlp_backward(step, both):
        grad_outs[step] = both
        grad_inner = matmul(both, down_w)
        pull = jax.vjp(
            lambda gate_in, up_in: jax.nn.gelu(gate_in, approximate=True) * up_in,
            gates[step],
            ups[step],
        )[1]
        grad_gate, grad_up = pull(grad_inner)
        grad_gates[step] = grad_gate.astype(bf16)
        grad_ups[step] = grad_up.astype(bf16)
        return matmul_rt(grad_gates[step], gate_w) + matmul_rt(grad_ups[step], up_w)

    def blocks_back(got):
        return jnp.concatenate([got[i] for i in range(z_size)], axis=1).astype(f32)

    def reduce_terms(full):
        full = full.reshape(z_size, y_size, 2, part, block)

        def of_core(which):
            return lax.dynamic_slice_in_dim(full, which, 1, 2)[:, :, 0].transpose(1, 0, 2, 3)

        halves = by_core(of_core(core), core_swap(of_core(1 - core)))
        return jnp.stack(halves, axis=1).reshape((y_size * 2 * z_size,) + full.shape[3:])

    def reduce(every):
        return lax.psum_scatter(
            every, ("ctx", "tp"), scatter_dimension=0, tiled=True, axis_index_groups=same_core
        )

    def joined(pieces):
        return jnp.concatenate([pieces[step] for step in range(z_size)], axis=0)

    down_terms = []

    def before_last():
        grad_down_w = matmul_lt(joined(grad_outs), joined(inners)).astype(bf16)
        down_terms.append(reduce_terms(grad_down_w))
        return down_terms[0]

    grad_three, lows = ring_rows(grad_mlp.astype(bf16), mlp_backward, before_last, True)
    down_sum = reduce(down_terms[0])
    all_in = joined(mlp_in)
    grad_gate_w = matmul_lt(tie(all_in, lows[2]), joined(grad_gates)).astype(bf16)
    gate_terms = reduce_terms(grad_gate_w)
    gate_sum = reduce(gate_terms)
    grad_three = tie(grad_three, gate_terms)

    grad_middle = grad_result + norm_back(grad_three, normal_three, inverse_three)
    grad_post_attn = jnp.sum(grad_middle * normal_two, axis=0)
    grad_branch = norm_back(grad_middle * post_attn, normal_two, inverse_two).astype(bf16)
    grad_up_w = matmul_lt(tie(all_in, grad_branch), joined(grad_ups)).astype(bf16)
    up_terms = reduce_terms(grad_up_w)
    up_sum = reduce(up_terms)
    down_got = over_z(tie(down_sum, grad_branch))
    branch_rows = rows_of(grad_branch, tie(tp_swap(grad_branch), up_terms, down_got))
    post_terms = jnp.stack([grad_post_attn, grad_post_mlp], axis=0)
    post_terms = post_terms.reshape(2, z_size, y_size, 2, part).transpose(1, 2, 3, 0, 4)
    post_y = scatter_y(post_terms)
    branch_rows = tie(branch_rows, post_y)
    post_z = scatter_z(post_y)
    branch_chip = jnp.concatenate([branch_rows, core_swap(branch_rows)], axis=0)
    grad_attn = matmul(branch_chip, out_w).astype(bf16)
    grad_out_w = matmul_lt(tie(branch_chip, grad_attn), attn_out).astype(bf16)
    out_y = scatter_y(grad_out_w.reshape(z_size, y_size, 2 * part, q_cols)).astype(bf16)
    grad_heads = jnp.stack(
        [grad_attn[:, i * HD : (i + 1) * HD] for i in range(shared_by)], axis=0
    ).reshape(shared_by, 2, rows, HD)
    prompt_gq, prompt_gk, prompt_gv = attend_backward(
        prompt_query,
        own_kv[:, :HD],
        own_kv[:, HD:],
        prompt_allowed,
        prompt_total,
        grad_heads[:, :, :prompt_local].reshape(-1, HD),
    )
    prompt_gkv = jnp.concatenate([prompt_gk, prompt_gv], axis=1)
    gate_got = over_z(tie(gate_sum, grad_attn))
    grad_heads = tie(grad_heads, gate_got, *post_z)
    cont_gq, cont_gkv, own_gkv = [], [], []
    for i in range(2 * cont_count):
        at = prompt_local + (i % cont_count) * cont_size
        half = i // cont_count
        query, kv, _, total = conts[i]
        gq, gk, gv = attend_backward(
            query,
            kv[:, :HD],
            kv[:, HD:],
            cont_allowed,
            total,
            grad_heads[:, half, at : at + cont_size].reshape(-1, HD),
        )
        cont_gq.append(gq.reshape(shared_by, cont_size, HD))
        gkv = jnp.concatenate([gk, gv], axis=1)
        cont_gkv.append(gkv[:span])
        own_gkv.append(gkv[span:])

    def kv_take(z_at, y_at):
        length = 2 * prompt_local

        def piece(values):
            return lax.dynamic_slice_in_dim(values, y_at * length, length, 0)

        total = jnp.where(z_at == z, piece(prompt_gkv), 0.0)
        for which, term in zip(which_prompt, cont_gkv):
            total = total + jnp.where(z_at == which, piece(term), 0.0)
        return total

    out_got = over_z(out_y)
    up_got = over_z(tie(up_sum, out_got))
    kv_terms, kv_total = scatter_grid(kv_take, pairs, (out_y, up_got))
    grad_q = rows_order(prompt_gq.reshape(shared_by, 2, prompt_local, HD), cont_gq)
    grad_q_proj = jnp.concatenate(
        [
            rotary(grad_q[:, i * HD : (i + 1) * HD] * query_scale, cosine, -sine_wave)
            for i in range(shared_by)
        ],
        axis=1,
    ).astype(bf16)
    grad_q_w = matmul_lt(chip_rows, grad_q_proj).astype(bf16)
    q_y = scatter_y(tie(grad_q_w, kv_total).reshape(z_size, y_size, 2 * part, q_cols))
    kv_low = add_up(tie(kv_terms, q_y))
    kv_sum = kv_low.reshape(2, prompt_local, 2 * HD)
    halves = []
    for half in range(2):
        halves.append(kv_sum[half])
        halves.extend(own_gkv[half * cont_count : (half + 1) * cont_count])
    grad_kv = jnp.concatenate(halves, axis=0)
    grad_kv_proj = jnp.concatenate(
        [rotary(grad_kv[:, :HD], cosine, -sine_wave), grad_kv[:, HD:]], axis=1
    ).astype(bf16)
    one_partial = matmul_rt(grad_q_proj, attn_w[:, :q_cols]) + matmul_rt(
        grad_kv_proj, attn_w[:, q_cols:]
    )
    one_core = one_partial[:rows] + core_swap(one_partial[rows:].astype(bf16)).astype(f32)
    one_give = give_share(one_core).astype(bf16)
    one_got = tp_swap(one_give)
    grad_kv_w = matmul_lt(tie(chip_rows, one_give), grad_kv_proj).astype(bf16)
    kvw_y = scatter_y(grad_kv_w.reshape(z_size, y_size, 2 * part, 2 * kv_cols))
    q_got = over_z(tie(q_y, one_give).astype(bf16))
    one_got = tie(one_got, q_got)
    grad_one = take_share(one_core) + one_got.astype(f32)
    grad_input = grad_middle + norm_back(grad_one, take_share(normal_one), take_share(inverse_one))
    input_low = grad_input.astype(bf16)
    kvw_got = over_z(kvw_y.astype(bf16))
    raw_down = blocks_back(tie(down_got, input_low))
    raw_gate = blocks_back(tie(gate_got, input_low))
    raw_up = blocks_back(tie(up_got, input_low))
    out_sum = jnp.sum(tie(out_got, input_low).astype(f32), axis=0)
    q_sum = jnp.sum(tie(q_got, input_low).astype(f32), axis=0)
    kvw_sum = jnp.sum(tie(kvw_got, input_low).astype(f32), axis=0)
    post_sum = add_up(post_z)
    input_rows = rows_of(input_low, tp_swap(input_low)).astype(f32)

    def split_core(summed):
        mine = lax.dynamic_slice_in_dim(summed, core * part, part, 0)
        give = lax.dynamic_slice_in_dim(summed, (1 - core) * part, part, 0).astype(bf16)
        return mine, core_swap(give).astype(f32)

    grad_out = jnp.concatenate(by_core(*split_core(out_sum)), axis=1).T
    post_sum = row_of(post_sum, core) + core_swap(row_of(post_sum, 1 - core))
    raw_q = jnp.concatenate(by_core(*split_core(q_sum)), axis=1)
    first, second = by_core(*split_core(kvw_sum))
    raw_k = jnp.concatenate([first[:, :kv_cols], second[:, :kv_cols]], axis=1)
    raw_v = jnp.concatenate([first[:, kv_cols:], second[:, kv_cols:]], axis=1)

    def gain_sum(raw, weight):
        return jnp.sum(raw * weight.astype(f32), axis=1)

    gain_terms = jnp.stack(
        [
            gain_sum(raw_q, w_query) + gain_sum(raw_k, w_key) + gain_sum(raw_v, w_value),
            post_sum[0],
            gain_sum(raw_gate, w_gate) + gain_sum(raw_up, w_up),
            post_sum[1],
        ],
        axis=0,
    )
    gain_grads = gain_terms + tp_swap(gain_terms)

    return (
        result_rows[:prompt_local].reshape(1, prompt_local, width),
        result_rows[prompt_local:].reshape(cont_count, cont_size, width),
        input_rows[:prompt_local].reshape(1, prompt_local, width),
        input_rows[prompt_local:].reshape(cont_count, cont_size, width),
        gain_grads[0],
        gain_grads[1],
        gain_grads[2],
        gain_grads[3],
        raw_q * gain_one,
        raw_k * gain_one,
        raw_v * gain_one,
        grad_out,
        raw_gate * gain_three,
        raw_up * gain_three,
        raw_down.T,
    )


def solution(mesh):
    in_specs = (
        P("fsdp", "ctx", None),
        P(("fsdp", "ctx"), None, None),
        P(("fsdp", "ctx")),
        P(("fsdp", "ctx")),
        P(("fsdp", "ctx")),
        P(("fsdp", "ctx")),
        P(("fsdp", "ctx")),
        P(("fsdp", "ctx")),
        P(("fsdp", "ctx"), "tp"),
        P(("fsdp", "ctx"), "tp"),
        P(("fsdp", "ctx"), "tp"),
        P("tp", ("fsdp", "ctx")),
        P(("fsdp", "ctx"), "tp"),
        P(("fsdp", "ctx"), "tp"),
        P("tp", ("fsdp", "ctx")),
        P("fsdp", "ctx", None),
        P(("fsdp", "ctx"), None, None),
    )
    out_specs = (
        P("fsdp", "ctx", None),
        P(("fsdp", "ctx"), None, None),
        P("fsdp", "ctx", None),
        P(("fsdp", "ctx"), None, None),
        P(("fsdp", "ctx")),
        P(("fsdp", "ctx")),
        P(("fsdp", "ctx")),
        P(("fsdp", "ctx")),
        P(("fsdp", "ctx"), "tp"),
        P(("fsdp", "ctx"), "tp"),
        P(("fsdp", "ctx"), "tp"),
        P("tp", ("fsdp", "ctx")),
        P(("fsdp", "ctx"), "tp"),
        P(("fsdp", "ctx"), "tp"),
        P("tp", ("fsdp", "ctx")),
    )
    return jax.shard_map(shards, mesh=mesh, in_specs=in_specs, out_specs=out_specs, check_vma=False)
```

```python
import math

import jax
import jax.numpy as jnp
from jax import lax
from jax.sharding import PartitionSpec as P

HD = 256
PROMPT = 1024

soft_cap = 50.0
norm_eps = 1e-06
masked_fill = -1e30
bf16 = jnp.bfloat16
f32 = jnp.float32


def norm_parts(values):
    inverse = lax.rsqrt(jnp.mean(values * values, axis=-1, keepdims=True) + norm_eps)
    return (values * inverse, inverse)


def norm_back(grad_normal, normal, inverse):
    return inverse * (
        grad_normal - normal * jnp.mean(grad_normal * normal, axis=-1, keepdims=True)
    )


def rotary_tables(places, head_dim):
    half_dim = head_dim // 2
    frequency = jnp.exp(
        jnp.arange(half_dim, dtype=f32) * (-2.0 * math.log(10000.0) / head_dim)
    )
    angles = places[:, None] * frequency[None, :]
    return (jnp.cos(angles), jnp.sin(angles))


def rotary(values, cosine, sine_wave):
    half_dim = values.shape[-1] // 2
    front_half = values[..., :half_dim]
    back_half = values[..., half_dim:]
    return jnp.concatenate(
        [front_half * cosine - back_half * sine_wave, back_half * cosine + front_half * sine_wave],
        axis=-1,
    )


def tie(first, *others):
    return lax.optimization_barrier((first,) + others)[0]


def matmul(left, right):
    return jnp.dot(left, right, preferred_element_type=f32)


def matmul_rt(left, right):
    return lax.dot_general(left, right, (((1,), (1,)), ((), ())), preferred_element_type=f32)


def matmul_lt(left, right):
    return lax.dot_general(left, right, (((0,), (0,)), ((), ())), preferred_element_type=f32)


def attend_forward(query, key, value, allowed):
    raw_scores = matmul_rt(query, key)
    capped = jnp.where(allowed, soft_cap * jnp.tanh(raw_scores / soft_cap), masked_fill)
    row_peak = jnp.max(capped, axis=-1, keepdims=True)
    exponent = jnp.exp(capped - row_peak)
    row_total = jnp.sum(exponent, axis=-1, keepdims=True)
    weight_set = (exponent / row_total).astype(bf16)
    return (matmul(weight_set, value), row_peak + jnp.log(row_total))


def attend_backward(query, key, value, allowed, log_total, grad_mixed):
    raw_scores = matmul_rt(query, key)
    squashed = jnp.tanh(raw_scores / soft_cap)
    capped = jnp.where(allowed, soft_cap * squashed, masked_fill)
    probabilities = jnp.exp(capped - log_total)
    weight_set = probabilities.astype(bf16)
    grad_value = matmul_lt(weight_set, grad_mixed)
    grad_probs = matmul_rt(grad_mixed, value)
    inner_sum = jnp.sum(probabilities * grad_probs, axis=-1, keepdims=True)
    grad_scores = (probabilities * (grad_probs - inner_sum) * (1.0 - squashed * squashed)).astype(
        bf16
    )
    return (matmul(grad_scores, key), matmul_lt(grad_scores, query), grad_value)


def shards(
    prompt_x,
    cont_x,
    cont_prompt,
    cont_len,
    attn_norm,
    attn_post,
    mlp_norm,
    mlp_post,
    w_query,
    w_key,
    w_value,
    w_out,
    w_gate,
    w_up,
    w_down,
    prompt_cot,
    cont_cot,
):
    width = prompt_x.shape[2]
    prompt_local = prompt_x.shape[1]
    cont_count = cont_x.shape[0]
    cont_size = cont_x.shape[1]
    cont_rows = cont_count * cont_size
    rows = prompt_local + cont_rows
    z_size = lax.axis_size("fsdp")
    c_size = lax.axis_size("ctx")
    y_size = c_size // 2
    z = lax.axis_index("fsdp")
    c = lax.axis_index("ctx")
    y = c // 2
    core = c % 2
    t = lax.axis_index("tp")
    part = w_query.shape[0]
    q_cols = w_query.shape[1] // 2
    kv_cols = w_key.shape[1] // 2
    shared_by = q_cols // kv_cols
    a_cols = q_cols + 2 * kv_cols
    block = w_gate.shape[1] // z_size
    share = rows // 2
    query_scale = HD ** (-0.5)

    def z_shift(values, step):
        return lax.ppermute(values, "fsdp", [(i, (i + step) % z_size) for i in range(z_size)])

    def y_next(values):
        return lax.ppermute(values, "ctx", [(i, (i + 2) % c_size) for i in range(c_size)])

    def core_swap(values):
        return lax.ppermute(values, "ctx", [(i, i ^ 1) for i in range(c_size)])

    def tp_swap(values):
        return lax.ppermute(values, "tp", [(0, 1), (1, 0)])

    def by_core(own, other):
        return (jnp.where(core == 0, own, other), jnp.where(core == 0, other, own))

    def place(held, piece, *index):
        piece = piece.reshape((1,) * len(index) + piece.shape)
        return lax.dynamic_update_slice(held, piece, index + (0,) * (held.ndim - len(index)))

    def gather_grid(own, waits=()):
        held = jnp.zeros((z_size, y_size) + own.shape, own.dtype)
        chunk, arrivals, extra = own, [], list(waits)
        for step in range(z_size):
            if step:
                chunk = tie(ahead, turn)
            ahead = z_shift(chunk, 1) if step < z_size - 1 else None
            if ahead is not None:
                arrivals.append(ahead)
            elif step:
                arrivals[-1] = chunk
            turn = chunk
            for hop in range(y_size):
                if hop:
                    turn = y_next(turn)
                held = place(held, turn, (z - step) % z_size, (y - hop) % y_size)
        return held, arrivals, turn

    def row_of(values, at):
        return lax.dynamic_slice_in_dim(values, at, 1, 0)[0]

    def scatter_y(values):
        def column(at):
            return lax.dynamic_slice_in_dim(values, at, 1, 1)[:, 0].astype(f32)

        total = column((y - 1) % y_size)
        for hop in range(2, y_size + 1):
            total = y_next(total.astype(bf16)).astype(f32) + column((y - hop) % y_size)
        return total

    def scatter_z(values):
        low = values.astype(bf16)
        terms = [row_of(values, z)]
        for step in range(1, z_size):
            terms.append(z_shift(row_of(low, (z + step) % z_size), step))
        return terms

    def add_up(terms):
        total = terms[0].astype(f32)
        for term in terms[1:]:
            total = total + term.astype(f32)
        return total

    def scatter_grid(take, groups, waits=()):
        steps, sent = list(range(1, z_size)) + [0], {}
        for size in groups:
            now, steps = steps[:size], steps[size:]

            def terms(y_at):
                return jnp.stack([take((z + step) % z_size, y_at) for step in now], axis=0)

            total = terms((y - 1) % y_size)
            for hop in range(2, y_size + 1):
                total = y_next(total.astype(bf16)).astype(f32) + terms((y - hop) % y_size)
            if waits:
                total, waits = tie(total, waits[0]), waits[1:]
            for i, step in enumerate(now):
                sent[step] = z_shift(total[i].astype(bf16), step) if step else total[i]
        return [sent[step] for step in range(z_size)], total

    def taker(values):
        tail = (0,) * (values.ndim - 2)

        def take(z_at, y_at):
            piece = lax.dynamic_slice(values, (z_at, y_at) + tail, (1, 1) + values.shape[2:])
            return piece[0, 0].astype(f32)

        return take

    def take_share(values):
        return lax.dynamic_slice_in_dim(values, t * share, share, 0)

    def give_share(values):
        return lax.dynamic_slice_in_dim(values, (1 - t) * share, share, 0)

    def rows_of(mine, other):
        return jnp.concatenate(
            [jnp.where(t == 0, mine, other), jnp.where(t == 0, other, mine)], axis=0
        )

    gain_one = attn_norm.astype(f32)[:, None]
    gain_three = mlp_norm.astype(f32)[:, None]
    pairs = (2,) * (z_size // 2)
    same_core = [[y_at * 2 * 2 + which * 2 + t_at for y_at in range(y_size) for t_at in range(2)] for which in range(2)]

    def over_z(values):
        return lax.all_to_all(values, "fsdp", 0, 0, tiled=True)

    def z_blocks(local):
        return jnp.stack([local[:, i * block : (i + 1) * block] for i in range(z_size)], axis=0)

    scaled_q = (w_query.astype(f32) * gain_one).astype(bf16)
    scaled_k = (w_key.astype(f32) * gain_one).astype(bf16)
    scaled_v = (w_value.astype(f32) * gain_one).astype(bf16)

    gains = jnp.concatenate(
        [attn_post[:, None], mlp_post[:, None], jnp.zeros((part, 126), bf16)], axis=1
    )

    def head_cols(which):
        return jnp.concatenate(
            [
                lax.dynamic_slice_in_dim(scaled_q, which * q_cols, q_cols, 1),
                lax.dynamic_slice_in_dim(scaled_k, which * kv_cols, kv_cols, 1),
                lax.dynamic_slice_in_dim(scaled_v, which * kv_cols, kv_cols, 1),
                lax.dynamic_slice_in_dim(w_out.T, which * q_cols, q_cols, 1),
                gains,
            ],
            axis=1,
        )

    mine, other = by_core(head_cols(core), core_swap(head_cols(1 - core)))
    attn_own = jnp.stack([mine, other], axis=0)
    gate_low = z_blocks((w_gate.astype(f32) * gain_three).astype(bf16))
    up_low = z_blocks((w_up.astype(f32) * gain_three).astype(bf16))
    down_low = z_blocks(w_down.T)
    attn_grid, _, attn_y = gather_grid(attn_own)
    gate_held = over_z(tie(gate_low, attn_y))
    attn_grid = attn_grid.reshape(width, a_cols + q_cols + 128)
    attn_w = attn_grid[:, :a_cols]
    out_w = attn_grid[:, a_cols : a_cols + q_cols]
    prompt_x, cont_x = tie((prompt_x, cont_x), attn_own)

    def spread(held):
        return lax.all_gather(
            held, ("ctx", "tp"), axis=0, tiled=False, axis_index_groups=same_core
        ).reshape((y_size, 2) + held.shape)

    def spread_end(every):
        mine = lax.dynamic_slice_in_dim(every, core, 1, 1)[:, 0]
        got = core_swap(lax.dynamic_slice_in_dim(every, 1 - core, 1, 1)[:, 0])
        full = jnp.zeros((z_size, y_size, 2, part, block), bf16)
        for which, rows_at in ((core, mine), (1 - core, got)):
            full = lax.dynamic_update_slice(
                full, rows_at.transpose(1, 0, 2, 3)[:, :, None], (0, 0, which, 0, 0)
            )
        return full.reshape(width, block)

    gate_every = spread(gate_held)
    up_held = over_z(tie(up_low, gate_held))
    up_every = spread(up_held)

    residual = jnp.concatenate(
        [prompt_x.reshape(prompt_local, width), cont_x.reshape(cont_rows, width)], axis=0
    ).astype(f32)
    normal_one, inverse_one = norm_parts(residual)
    normal_low = normal_one.astype(bf16)
    chip_rows = jnp.concatenate([normal_low, core_swap(normal_low)], axis=0)

    core_of = (core, 1 - core)
    cont_places = PROMPT + jnp.tile(jnp.arange(cont_size, dtype=jnp.int32), cont_count)
    prompt_places = [
        (y * 2 + which) * prompt_local + jnp.arange(prompt_local, dtype=jnp.int32)
        for which in core_of
    ]
    places = jnp.concatenate(
        [prompt_places[0], cont_places, prompt_places[1], cont_places]
    ).astype(f32)
    cosine, sine_wave = rotary_tables(places, HD)
    projected = matmul(chip_rows, attn_w)
    query_rows = jnp.stack(
        [
            (rotary(projected[:, i * HD : (i + 1) * HD], cosine, sine_wave) * query_scale).astype(bf16)
            for i in range(shared_by)
        ],
        axis=0,
    ).reshape(shared_by, 2, rows, HD)
    key_rows = rotary(projected[:, q_cols : q_cols + HD], cosine, sine_wave).astype(bf16)
    value_rows = projected[:, q_cols + HD :].astype(bf16)
    kv_rows = jnp.concatenate([key_rows, value_rows], axis=1).reshape(2, rows, 2 * HD)
    prompt_kv = kv_rows[:, :prompt_local].reshape(2 * prompt_local, 2 * HD)
    every_kv, kv_z, kv_y = gather_grid(tie(prompt_kv, gate_held))
    every_kv = every_kv.reshape(z_size, y_size * 2 * prompt_local, 2 * HD)
    span = every_kv.shape[1]
    every_kv = tie(every_kv, up_held)
    down_held = over_z(tie(down_low, up_held))
    down_every = spread(down_held)
    own_kv = lax.dynamic_slice(every_kv, (z, 0, 0), (1, span, 2 * HD))[0]
    key_places = (
        (jnp.arange(y_size, dtype=jnp.int32)[:, None, None] * 2
         + jnp.stack(core_of)[None, :, None]) * prompt_local
        + jnp.arange(prompt_local, dtype=jnp.int32)[None, None, :]
    ).reshape(1, span)
    head_places = jnp.tile(jnp.concatenate(prompt_places), shared_by)
    prompt_allowed = key_places <= head_places[:, None]
    cont_allowed = jnp.tile(
        jnp.arange(span + cont_size, dtype=jnp.int32)[None, :]
        <= span + jnp.arange(cont_size, dtype=jnp.int32)[:, None],
        (shared_by, 1),
    )
    prompt_query = query_rows[:, :, :prompt_local].reshape(-1, HD)
    prompt_mixed, prompt_total = attend_forward(
        prompt_query, own_kv[:, :HD], own_kv[:, HD:], prompt_allowed
    )
    prompt_mixed = prompt_mixed.astype(bf16).reshape(shared_by, 2, prompt_local, HD)
    other_prompt = core_swap(cont_prompt)
    which_prompt = [cont_prompt[i] for i in range(cont_count)] + [
        other_prompt[i] for i in range(cont_count)
    ]
    conts = []
    for i in range(2 * cont_count):
        at = prompt_local + (i % cont_count) * cont_size
        half = i // cont_count
        kv = jnp.concatenate(
            [
                lax.dynamic_slice(every_kv, (which_prompt[i], 0, 0), (1, span, 2 * HD))[0],
                kv_rows[half, at : at + cont_size],
            ],
            axis=0,
        )
        query = query_rows[:, half, at : at + cont_size].reshape(-1, HD)
        mixed, total = attend_forward(query, kv[:, :HD], kv[:, HD:], cont_allowed)
        conts.append((query, kv, mixed.astype(bf16).reshape(shared_by, cont_size, HD), total))

    def rows_order(prompt_part, cont_parts):
        halves = []
        for half in range(2):
            pieces = [prompt_part[:, half]] + cont_parts[half * cont_count : (half + 1) * cont_count]
            halves.append(jnp.concatenate(pieces, axis=1))
        heads = jnp.concatenate(halves, axis=1)
        return jnp.concatenate([heads[i] for i in range(shared_by)], axis=1)

    attn_out = rows_order(prompt_mixed, [entry[2] for entry in conts])

    def to_shares(partial):
        low = partial.astype(bf16)
        summed = partial[:rows] + core_swap(low[rows:]).astype(f32)
        return take_share(summed) + tp_swap(give_share(summed).astype(bf16)).astype(f32)

    pick = (
        jnp.arange(8, dtype=jnp.int32)[:, None] == jnp.arange(128, dtype=jnp.int32)[None, :]
    ).astype(bf16)
    post_rows = matmul_rt(pick, attn_grid[:, a_cols + q_cols :])
    post_attn, post_mlp = post_rows[0:1], post_rows[1:2]
    branch_partial = matmul_rt(tie(attn_out, down_held), out_w)
    branch_core = branch_partial[:rows] + core_swap(branch_partial[rows:].astype(bf16)).astype(f32)
    branch_give = give_share(branch_core).astype(bf16)
    branch_got = tp_swap(branch_give)
    gate_w = spread_end(tie(gate_every, branch_give))
    branch = take_share(branch_core) + tie(branch_got, gate_w).astype(f32)
    up_w = spread_end(up_every)

    normal_two, inverse_two = norm_parts(branch)
    middle = take_share(residual) + normal_two * post_attn
    normal_three, inverse_three = norm_parts(middle)

    three_low = normal_three.astype(bf16)
    down_w = spread_end(tie(down_every, three_low))

    def ring_rows(own, step_fn, before_last=None, own_first=False):
        sums = []
        chunk = own
        for step in range(z_size):
            if step:
                chunk = z_shift(chunk, 1)
            if step == 1 and own_first:
                chunk = tie(chunk, partial)
            both = jnp.concatenate([chunk, core_swap(chunk)], axis=0)
            partial = step_fn(step, both)
            sums.append(
                partial[:share] + core_swap(partial[share:].astype(bf16)).astype(f32)
            )
        total, lows = sums[1], []
        for step in list(range(2, z_size)) + [0]:
            lows.append(total.astype(bf16))
            if step == 0 and before_last is not None:
                lows[-1] = tie(lows[-1], before_last())
            total = z_shift(lows[-1], 1).astype(f32) + sums[step]
        return total, lows

    mlp_in, gates, ups, inners = {}, {}, {}, {}

    def mlp_forward(step, both):
        mlp_in[step] = both
        gates[step] = matmul(both, gate_w)
        ups[step] = matmul(both, up_w)
        inners[step] = (jax.nn.gelu(gates[step], approximate=True) * ups[step]).astype(bf16)
        return matmul_rt(inners[step], down_w)

    mlp_share, _ = ring_rows(three_low, mlp_forward)

    normal_four, inverse_four = norm_parts(mlp_share)
    cont_live = (
        (jnp.arange(cont_size, dtype=jnp.int32)[None, :] < cont_len[:, None])
        .astype(f32)
        .reshape(cont_rows)
    )
    live_rows = jnp.concatenate([jnp.ones((prompt_local,), f32), cont_live])
    live = take_share(live_rows)[:, None]
    result_share = ((middle + normal_four * post_mlp) * live).astype(bf16)
    result_rows = rows_of(result_share, tp_swap(result_share))
    cot_rows = jnp.concatenate(
        [prompt_cot.reshape(prompt_local, width), cont_cot.reshape(cont_rows, width)], axis=0
    )
    grad_result = take_share(cot_rows).astype(f32) * live
    grad_post_mlp = jnp.sum(grad_result * normal_four, axis=0)
    grad_mlp = norm_back(grad_result * post_mlp, normal_four, inverse_four)

    grad_outs, grad_gates, grad_ups = {}, {}, {}

    def mlp_backward(step, both):
        grad_outs[step] = both
        grad_inner = matmul(both, down_w)
        pull = jax.vjp(
            lambda gate_in, up_in: jax.nn.gelu(gate_in, approximate=True) * up_in,
            gates[step],
            ups[step],
        )[1]
        grad_gate, grad_up = pull(grad_inner)
        grad_gates[step] = grad_gate.astype(bf16)
        grad_ups[step] = grad_up.astype(bf16)
        return matmul_rt(grad_gates[step], gate_w) + matmul_rt(grad_ups[step], up_w)

    def blocks_back(got):
        return jnp.concatenate([got[i] for i in range(z_size)], axis=1).astype(f32)

    def reduce_terms(full):
        full = full.reshape(z_size, y_size, 2, part, block)

        def of_core(which):
            return lax.dynamic_slice_in_dim(full, which, 1, 2)[:, :, 0].transpose(1, 0, 2, 3)

        halves = by_core(of_core(core), core_swap(of_core(1 - core)))
        return jnp.stack(halves, axis=1).reshape((y_size * 2 * z_size,) + full.shape[3:])

    def reduce(every):
        return lax.psum_scatter(
            every, ("ctx", "tp"), scatter_dimension=0, tiled=True, axis_index_groups=same_core
        )

    def joined(pieces):
        return jnp.concatenate([pieces[step] for step in range(z_size)], axis=0)

    down_terms = []

    def before_last():
        grad_down_w = matmul_lt(joined(grad_outs), joined(inners)).astype(bf16)
        down_terms.append(reduce_terms(grad_down_w))
        return down_terms[0]

    grad_three, lows = ring_rows(grad_mlp.astype(bf16), mlp_backward, before_last, True)
    down_sum = reduce(down_terms[0])
    all_in = joined(mlp_in)
    grad_gate_w = matmul_lt(tie(all_in, lows[2]), joined(grad_gates)).astype(bf16)
    gate_terms = reduce_terms(grad_gate_w)
    gate_sum = reduce(gate_terms)
    grad_three = tie(grad_three, gate_terms)

    grad_middle = grad_result + norm_back(grad_three, normal_three, inverse_three)
    grad_post_attn = jnp.sum(grad_middle * normal_two, axis=0)
    grad_branch = norm_back(grad_middle * post_attn, normal_two, inverse_two).astype(bf16)
    grad_up_w = matmul_lt(tie(all_in, grad_branch), joined(grad_ups)).astype(bf16)
    up_terms = reduce_terms(grad_up_w)
    up_sum = reduce(up_terms)
    down_got = over_z(tie(down_sum, grad_branch))
    branch_rows = rows_of(grad_branch, tie(tp_swap(grad_branch), up_terms, down_got))
    post_terms = jnp.stack([grad_post_attn, grad_post_mlp], axis=0)
    post_terms = post_terms.reshape(2, z_size, y_size, 2, part).transpose(1, 2, 3, 0, 4)
    post_y = scatter_y(post_terms)
    branch_rows = tie(branch_rows, post_y)
    post_z = scatter_z(post_y)
    branch_chip = jnp.concatenate([branch_rows, core_swap(branch_rows)], axis=0)
    grad_attn = matmul(branch_chip, out_w).astype(bf16)
    grad_out_w = matmul_lt(tie(branch_chip, grad_attn), attn_out).astype(bf16)
    out_y = scatter_y(grad_out_w.reshape(z_size, y_size, 2 * part, q_cols)).astype(bf16)
    grad_heads = jnp.stack(
        [grad_attn[:, i * HD : (i + 1) * HD] for i in range(shared_by)], axis=0
    ).reshape(shared_by, 2, rows, HD)
    prompt_gq, prompt_gk, prompt_gv = attend_backward(
        prompt_query,
        own_kv[:, :HD],
        own_kv[:, HD:],
        prompt_allowed,
        prompt_total,
        grad_heads[:, :, :prompt_local].reshape(-1, HD),
    )
    prompt_gkv = jnp.concatenate([prompt_gk, prompt_gv], axis=1)
    gate_got = over_z(tie(gate_sum, grad_attn))
    grad_heads = tie(grad_heads, gate_got, *post_z)
    cont_gq, cont_gkv, own_gkv = [], [], []
    for i in range(2 * cont_count):
        at = prompt_local + (i % cont_count) * cont_size
        half = i // cont_count
        query, kv, _, total = conts[i]
        gq, gk, gv = attend_backward(
            query,
            kv[:, :HD],
            kv[:, HD:],
            cont_allowed,
            total,
            grad_heads[:, half, at : at + cont_size].reshape(-1, HD),
        )
        cont_gq.append(gq.reshape(shared_by, cont_size, HD))
        gkv = jnp.concatenate([gk, gv], axis=1)
        cont_gkv.append(gkv[:span])
        own_gkv.append(gkv[span:])

    def kv_take(z_at, y_at):
        length = 2 * prompt_local

        def piece(values):
            return lax.dynamic_slice_in_dim(values, y_at * length, length, 0)

        total = jnp.where(z_at == z, piece(prompt_gkv), 0.0)
        for which, term in zip(which_prompt, cont_gkv):
            total = total + jnp.where(z_at == which, piece(term), 0.0)
        return total

    out_got = over_z(out_y)
    up_got = over_z(tie(up_sum, out_got))
    kv_terms, kv_total = scatter_grid(kv_take, pairs, (out_y, up_got))
    grad_q = rows_order(prompt_gq.reshape(shared_by, 2, prompt_local, HD), cont_gq)
    grad_q_proj = jnp.concatenate(
        [
            rotary(grad_q[:, i * HD : (i + 1) * HD] * query_scale, cosine, -sine_wave)
            for i in range(shared_by)
        ],
        axis=1,
    ).astype(bf16)
    grad_q_w = matmul_lt(chip_rows, grad_q_proj).astype(bf16)
    q_y = scatter_y(tie(grad_q_w, kv_total).reshape(z_size, y_size, 2 * part, q_cols))
    kv_low = add_up(tie(kv_terms, q_y))
    kv_sum = kv_low.reshape(2, prompt_local, 2 * HD)
    halves = []
    for half in range(2):
        halves.append(kv_sum[half])
        halves.extend(own_gkv[half * cont_count : (half + 1) * cont_count])
    grad_kv = jnp.concatenate(halves, axis=0)
    grad_kv_proj = jnp.concatenate(
        [rotary(grad_kv[:, :HD], cosine, -sine_wave), grad_kv[:, HD:]], axis=1
    ).astype(bf16)
    one_partial = matmul_rt(grad_q_proj, attn_w[:, :q_cols]) + matmul_rt(
        grad_kv_proj, attn_w[:, q_cols:]
    )
    one_core = one_partial[:rows] + core_swap(one_partial[rows:].astype(bf16)).astype(f32)
    one_give = give_share(one_core).astype(bf16)
    one_got = tp_swap(one_give)
    grad_kv_w = matmul_lt(tie(chip_rows, one_give), grad_kv_proj).astype(bf16)
    kvw_y = scatter_y(grad_kv_w.reshape(z_size, y_size, 2 * part, 2 * kv_cols))
    q_got = over_z(tie(q_y, one_give).astype(bf16))
    one_got = tie(one_got, q_got)
    grad_one = take_share(one_core) + one_got.astype(f32)
    grad_input = grad_middle + norm_back(grad_one, take_share(normal_one), take_share(inverse_one))
    input_low = grad_input.astype(bf16)
    kvw_got = over_z(kvw_y.astype(bf16))
    raw_down = blocks_back(tie(down_got, input_low))
    raw_gate = blocks_back(tie(gate_got, input_low))
    raw_up = blocks_back(tie(up_got, input_low))
    out_sum = jnp.sum(tie(out_got, input_low).astype(f32), axis=0)
    q_sum = jnp.sum(tie(q_got, input_low).astype(f32), axis=0)
    kvw_sum = jnp.sum(tie(kvw_got, input_low).astype(f32), axis=0)
    post_sum = add_up(post_z)
    input_rows = rows_of(input_low, tp_swap(input_low)).astype(f32)

    def split_core(summed):
        mine = lax.dynamic_slice_in_dim(summed, core * part, part, 0)
        give = lax.dynamic_slice_in_dim(summed, (1 - core) * part, part, 0).astype(bf16)
        return mine, core_swap(give).astype(f32)

    grad_out = jnp.concatenate(by_core(*split_core(out_sum)), axis=1).T
    post_sum = row_of(post_sum, core) + core_swap(row_of(post_sum, 1 - core))
    raw_q = jnp.concatenate(by_core(*split_core(q_sum)), axis=1)
    first, second = by_core(*split_core(kvw_sum))
    raw_k = jnp.concatenate([first[:, :kv_cols], second[:, :kv_cols]], axis=1)
    raw_v = jnp.concatenate([first[:, kv_cols:], second[:, kv_cols:]], axis=1)

    def gain_sum(raw, weight):
        return jnp.sum(raw * weight.astype(f32), axis=1)

    gain_terms = jnp.stack(
        [
            gain_sum(raw_q, w_query) + gain_sum(raw_k, w_key) + gain_sum(raw_v, w_value),
            post_sum[0],
            gain_sum(raw_gate, w_gate) + gain_sum(raw_up, w_up),
            post_sum[1],
        ],
        axis=0,
    )
    gain_grads = gain_terms + tp_swap(gain_terms)

    return (
        result_rows[:prompt_local].reshape(1, prompt_local, width),
        result_rows[prompt_local:].reshape(cont_count, cont_size, width),
        input_rows[:prompt_local].reshape(1, prompt_local, width),
        input_rows[prompt_local:].reshape(cont_count, cont_size, width),
        gain_grads[0],
        gain_grads[1],
        gain_grads[2],
        gain_grads[3],
        raw_q * gain_one,
        raw_k * gain_one,
        raw_v * gain_one,
        grad_out,
        raw_gate * gain_three,
        raw_up * gain_three,
        raw_down.T,
    )


def solution(mesh):
    in_specs = (
        P("fsdp", "ctx", None),
        P(("fsdp", "ctx"), None, None),
        P(("fsdp", "ctx")),
        P(("fsdp", "ctx")),
        P(("fsdp", "ctx")),
        P(("fsdp", "ctx")),
        P(("fsdp", "ctx")),
        P(("fsdp", "ctx")),
        P(("fsdp", "ctx"), "tp"),
        P(("fsdp", "ctx"), "tp"),
        P(("fsdp", "ctx"), "tp"),
        P("tp", ("fsdp", "ctx")),
        P(("fsdp", "ctx"), "tp"),
        P(("fsdp", "ctx"), "tp"),
        P("tp", ("fsdp", "ctx")),
        P("fsdp", "ctx", None),
        P(("fsdp", "ctx"), None, None),
    )
    out_specs = (
        P("fsdp", "ctx", None),
        P(("fsdp", "ctx"), None, None),
        P("fsdp", "ctx", None),
        P(("fsdp", "ctx"), None, None),
        P(("fsdp", "ctx")),
        P(("fsdp", "ctx")),
        P(("fsdp", "ctx")),
        P(("fsdp", "ctx")),
        P(("fsdp", "ctx"), "tp"),
        P(("fsdp", "ctx"), "tp"),
        P(("fsdp", "ctx"), "tp"),
        P("tp", ("fsdp", "ctx")),
        P(("fsdp", "ctx"), "tp"),
        P(("fsdp", "ctx"), "tp"),
        P("tp", ("fsdp", "ctx")),
    )
    return jax.shard_map(shards, mesh=mesh, in_specs=in_specs, out_specs=out_specs, check_vma=False)
```

```python
import math

import jax
import jax.numpy as jnp
from jax import lax
from jax.sharding import PartitionSpec as P

HD = 256
PROMPT = 1024

soft_cap = 50.0
norm_eps = 1e-06
masked_fill = -1e30
bf16 = jnp.bfloat16
f32 = jnp.float32


def norm_parts(values):
    inverse = lax.rsqrt(jnp.mean(values * values, axis=-1, keepdims=True) + norm_eps)
    return (values * inverse, inverse)


def norm_back(grad_normal, normal, inverse):
    return inverse * (
        grad_normal - normal * jnp.mean(grad_normal * normal, axis=-1, keepdims=True)
    )


def rotary_tables(places, head_dim):
    half_dim = head_dim // 2
    frequency = jnp.exp(
        jnp.arange(half_dim, dtype=f32) * (-2.0 * math.log(10000.0) / head_dim)
    )
    angles = places[:, None] * frequency[None, :]
    return (jnp.cos(angles), jnp.sin(angles))


def rotary(values, cosine, sine_wave):
    half_dim = values.shape[-1] // 2
    front_half = values[..., :half_dim]
    back_half = values[..., half_dim:]
    return jnp.concatenate(
        [front_half * cosine - back_half * sine_wave, back_half * cosine + front_half * sine_wave],
        axis=-1,
    )


def tie(first, *others):
    return lax.optimization_barrier((first,) + others)[0]


def matmul(left, right):
    return jnp.dot(left, right, preferred_element_type=f32)


def matmul_rt(left, right):
    return lax.dot_general(left, right, (((1,), (1,)), ((), ())), preferred_element_type=f32)


def matmul_lt(left, right):
    return lax.dot_general(left, right, (((0,), (0,)), ((), ())), preferred_element_type=f32)


def attend_forward(query, key, value, allowed):
    raw_scores = matmul_rt(query, key)
    capped = jnp.where(allowed, soft_cap * jnp.tanh(raw_scores / soft_cap), masked_fill)
    row_peak = jnp.max(capped, axis=-1, keepdims=True)
    exponent = jnp.exp(capped - row_peak)
    row_total = jnp.sum(exponent, axis=-1, keepdims=True)
    weight_set = (exponent / row_total).astype(bf16)
    return (matmul(weight_set, value), row_peak + jnp.log(row_total))


def attend_backward(query, key, value, allowed, log_total, grad_mixed):
    raw_scores = matmul_rt(query, key)
    squashed = jnp.tanh(raw_scores / soft_cap)
    capped = jnp.where(allowed, soft_cap * squashed, masked_fill)
    probabilities = jnp.exp(capped - log_total)
    weight_set = probabilities.astype(bf16)
    grad_value = matmul_lt(weight_set, grad_mixed)
    grad_probs = matmul_rt(grad_mixed, value)
    inner_sum = jnp.sum(probabilities * grad_probs, axis=-1, keepdims=True)
    grad_scores = (probabilities * (grad_probs - inner_sum) * (1.0 - squashed * squashed)).astype(
        bf16
    )
    return (matmul(grad_scores, key), matmul_lt(grad_scores, query), grad_value)


def shards(
    prompt_x,
    cont_x,
    cont_prompt,
    cont_len,
    attn_norm,
    attn_post,
    mlp_norm,
    mlp_post,
    w_query,
    w_key,
    w_value,
    w_out,
    w_gate,
    w_up,
    w_down,
    prompt_cot,
    cont_cot,
):
    width = prompt_x.shape[2]
    prompt_local = prompt_x.shape[1]
    cont_count = cont_x.shape[0]
    cont_size = cont_x.shape[1]
    cont_rows = cont_count * cont_size
    rows = prompt_local + cont_rows
    z_size = lax.axis_size("fsdp")
    c_size = lax.axis_size("ctx")
    y_size = c_size // 2
    z = lax.axis_index("fsdp")
    c = lax.axis_index("ctx")
    y = c // 2
    core = c % 2
    t = lax.axis_index("tp")
    part = w_query.shape[0]
    q_cols = w_query.shape[1] // 2
    kv_cols = w_key.shape[1] // 2
    shared_by = q_cols // kv_cols
    a_cols = q_cols + 2 * kv_cols
    block = w_gate.shape[1] // z_size
    share = rows // 2
    query_scale = HD ** (-0.5)

    def z_shift(values, step):
        return lax.ppermute(values, "fsdp", [(i, (i + step) % z_size) for i in range(z_size)])

    def y_next(values):
        return lax.ppermute(values, "ctx", [(i, (i + 2) % c_size) for i in range(c_size)])

    def core_swap(values):
        return lax.ppermute(values, "ctx", [(i, i ^ 1) for i in range(c_size)])

    def tp_swap(values):
        return lax.ppermute(values, "tp", [(0, 1), (1, 0)])

    def by_core(own, other):
        return (jnp.where(core == 0, own, other), jnp.where(core == 0, other, own))

    def place(held, piece, *index):
        piece = piece.reshape((1,) * len(index) + piece.shape)
        return lax.dynamic_update_slice(held, piece, index + (0,) * (held.ndim - len(index)))

    def gather_grid(own, waits=()):
        held = jnp.zeros((z_size, y_size) + own.shape, own.dtype)
        chunk, arrivals, extra = own, [], list(waits)
        for step in range(z_size):
            if step:
                chunk = tie(ahead, turn)
            ahead = z_shift(chunk, 1) if step < z_size - 1 else None
            if ahead is not None:
                arrivals.append(ahead)
            elif step:
                arrivals[-1] = chunk
            turn = chunk
            for hop in range(y_size):
                if hop:
                    turn = y_next(turn)
                held = place(held, turn, (z - step) % z_size, (y - hop) % y_size)
        return held, arrivals, turn

    def row_of(values, at):
        return lax.dynamic_slice_in_dim(values, at, 1, 0)[0]

    def scatter_y(values):
        def column(at):
            return lax.dynamic_slice_in_dim(values, at, 1, 1)[:, 0].astype(f32)

        total = column((y - 1) % y_size)
        for hop in range(2, y_size + 1):
            total = y_next(total.astype(bf16)).astype(f32) + column((y - hop) % y_size)
        return total

    def scatter_z(values):
        low = values.astype(bf16)
        terms = [row_of(values, z)]
        for step in range(1, z_size):
            terms.append(z_shift(row_of(low, (z + step) % z_size), step))
        return terms

    def add_up(terms):
        total = terms[0].astype(f32)
        for term in terms[1:]:
            total = total + term.astype(f32)
        return total

    def scatter_grid(take, groups, waits=()):
        steps, sent = list(range(1, z_size)) + [0], {}
        for size in groups:
            now, steps = steps[:size], steps[size:]

            def terms(y_at):
                return jnp.stack([take((z + step) % z_size, y_at) for step in now], axis=0)

            total = terms((y - 1) % y_size)
            for hop in range(2, y_size + 1):
                total = y_next(total.astype(bf16)).astype(f32) + terms((y - hop) % y_size)
            if waits:
                total, waits = tie(total, waits[0]), waits[1:]
            for i, step in enumerate(now):
                sent[step] = z_shift(total[i].astype(bf16), step) if step else total[i]
        return [sent[step] for step in range(z_size)], total

    def taker(values):
        tail = (0,) * (values.ndim - 2)

        def take(z_at, y_at):
            piece = lax.dynamic_slice(values, (z_at, y_at) + tail, (1, 1) + values.shape[2:])
            return piece[0, 0].astype(f32)

        return take

    def take_share(values):
        return lax.dynamic_slice_in_dim(values, t * share, share, 0)

    def give_share(values):
        return lax.dynamic_slice_in_dim(values, (1 - t) * share, share, 0)

    def rows_of(mine, other):
        return jnp.concatenate(
            [jnp.where(t == 0, mine, other), jnp.where(t == 0, other, mine)], axis=0
        )

    gain_one = attn_norm.astype(f32)[:, None]
    gain_three = mlp_norm.astype(f32)[:, None]
    pairs = (2,) * (z_size // 2)
    same_core = [[y_at * 2 * 2 + which * 2 + t_at for y_at in range(y_size) for t_at in range(2)] for which in range(2)]

    def over_z(values):
        return lax.all_to_all(values, "fsdp", 0, 0, tiled=True)

    def z_blocks(local):
        return jnp.stack([local[:, i * block : (i + 1) * block] for i in range(z_size)], axis=0)

    scaled_q = (w_query.astype(f32) * gain_one).astype(bf16)
    scaled_k = (w_key.astype(f32) * gain_one).astype(bf16)
    scaled_v = (w_value.astype(f32) * gain_one).astype(bf16)

    gains = jnp.concatenate(
        [attn_post[:, None], mlp_post[:, None], jnp.zeros((part, 126), bf16)], axis=1
    )

    def head_cols(which):
        return jnp.concatenate(
            [
                lax.dynamic_slice_in_dim(scaled_q, which * q_cols, q_cols, 1),
                lax.dynamic_slice_in_dim(scaled_k, which * kv_cols, kv_cols, 1),
                lax.dynamic_slice_in_dim(scaled_v, which * kv_cols, kv_cols, 1),
                lax.dynamic_slice_in_dim(w_out.T, which * q_cols, q_cols, 1),
                gains,
            ],
            axis=1,
        )

    mine, other = by_core(head_cols(core), core_swap(head_cols(1 - core)))
    attn_own = jnp.stack([mine, other], axis=0)
    gate_low = z_blocks((w_gate.astype(f32) * gain_three).astype(bf16))
    up_low = z_blocks((w_up.astype(f32) * gain_three).astype(bf16))
    down_low = z_blocks(w_down.T)
    attn_grid, _, attn_y = gather_grid(attn_own)
    gate_held = over_z(tie(gate_low, attn_y))
    attn_grid = attn_grid.reshape(width, a_cols + q_cols + 128)
    attn_w = attn_grid[:, :a_cols]
    out_w = attn_grid[:, a_cols : a_cols + q_cols]
    prompt_x, cont_x = tie((prompt_x, cont_x), attn_own)

    def spread(held):
        return lax.all_gather(
            held, ("ctx", "tp"), axis=0, tiled=False, axis_index_groups=same_core
        ).reshape((y_size, 2) + held.shape)

    def spread_end(every):
        mine = lax.dynamic_slice_in_dim(every, core, 1, 1)[:, 0]
        got = core_swap(lax.dynamic_slice_in_dim(every, 1 - core, 1, 1)[:, 0])
        full = jnp.zeros((z_size, y_size, 2, part, block), bf16)
        for which, rows_at in ((core, mine), (1 - core, got)):
            full = lax.dynamic_update_slice(
                full, rows_at.transpose(1, 0, 2, 3)[:, :, None], (0, 0, which, 0, 0)
            )
        return full.reshape(width, block)

    gate_every = spread(gate_held)
    up_held = over_z(tie(up_low, gate_held))
    up_every = spread(up_held)

    residual = jnp.concatenate(
        [prompt_x.reshape(prompt_local, width), cont_x.reshape(cont_rows, width)], axis=0
    ).astype(f32)
    normal_one, inverse_one = norm_parts(residual)
    normal_low = normal_one.astype(bf16)
    chip_rows = jnp.concatenate([normal_low, core_swap(normal_low)], axis=0)

    core_of = (core, 1 - core)
    cont_places = PROMPT + jnp.tile(jnp.arange(cont_size, dtype=jnp.int32), cont_count)
    prompt_places = [
        (y * 2 + which) * prompt_local + jnp.arange(prompt_local, dtype=jnp.int32)
        for which in core_of
    ]
    places = jnp.concatenate(
        [prompt_places[0], cont_places, prompt_places[1], cont_places]
    ).astype(f32)
    cosine, sine_wave = rotary_tables(places, HD)
    projected = matmul(chip_rows, attn_w)
    query_rows = jnp.stack(
        [
            (rotary(projected[:, i * HD : (i + 1) * HD], cosine, sine_wave) * query_scale).astype(bf16)
            for i in range(shared_by)
        ],
        axis=0,
    ).reshape(shared_by, 2, rows, HD)
    key_rows = rotary(projected[:, q_cols : q_cols + HD], cosine, sine_wave).astype(bf16)
    value_rows = projected[:, q_cols + HD :].astype(bf16)
    kv_rows = jnp.concatenate([key_rows, value_rows], axis=1).reshape(2, rows, 2 * HD)
    prompt_kv = kv_rows[:, :prompt_local].reshape(2 * prompt_local, 2 * HD)
    every_kv, kv_z, kv_y = gather_grid(tie(prompt_kv, gate_held))
    every_kv = every_kv.reshape(z_size, y_size * 2 * prompt_local, 2 * HD)
    span = every_kv.shape[1]
    every_kv = tie(every_kv, up_held)
    down_held = over_z(tie(down_low, up_held))
    down_every = spread(down_held)
    own_kv = lax.dynamic_slice(every_kv, (z, 0, 0), (1, span, 2 * HD))[0]
    key_places = (
        (jnp.arange(y_size, dtype=jnp.int32)[:, None, None] * 2
         + jnp.stack(core_of)[None, :, None]) * prompt_local
        + jnp.arange(prompt_local, dtype=jnp.int32)[None, None, :]
    ).reshape(1, span)
    head_places = jnp.tile(jnp.concatenate(prompt_places), shared_by)
    prompt_allowed = key_places <= head_places[:, None]
    cont_allowed = jnp.tile(
        jnp.arange(span + cont_size, dtype=jnp.int32)[None, :]
        <= span + jnp.arange(cont_size, dtype=jnp.int32)[:, None],
        (shared_by, 1),
    )
    prompt_query = query_rows[:, :, :prompt_local].reshape(-1, HD)
    prompt_mixed, prompt_total = attend_forward(
        prompt_query, own_kv[:, :HD], own_kv[:, HD:], prompt_allowed
    )
    prompt_mixed = prompt_mixed.astype(bf16).reshape(shared_by, 2, prompt_local, HD)
    other_prompt = core_swap(cont_prompt)
    which_prompt = [cont_prompt[i] for i in range(cont_count)] + [
        other_prompt[i] for i in range(cont_count)
    ]
    conts = []
    for i in range(2 * cont_count):
        at = prompt_local + (i % cont_count) * cont_size
        half = i // cont_count
        kv = jnp.concatenate(
            [
                lax.dynamic_slice(every_kv, (which_prompt[i], 0, 0), (1, span, 2 * HD))[0],
                kv_rows[half, at : at + cont_size],
            ],
            axis=0,
        )
        query = query_rows[:, half, at : at + cont_size].reshape(-1, HD)
        mixed, total = attend_forward(query, kv[:, :HD], kv[:, HD:], cont_allowed)
        conts.append((query, kv, mixed.astype(bf16).reshape(shared_by, cont_size, HD), total))

    def rows_order(prompt_part, cont_parts):
        halves = []
        for half in range(2):
            pieces = [prompt_part[:, half]] + cont_parts[half * cont_count : (half + 1) * cont_count]
            halves.append(jnp.concatenate(pieces, axis=1))
        heads = jnp.concatenate(halves, axis=1)
        return jnp.concatenate([heads[i] for i in range(shared_by)], axis=1)

    attn_out = rows_order(prompt_mixed, [entry[2] for entry in conts])

    def to_shares(partial):
        low = partial.astype(bf16)
        summed = partial[:rows] + core_swap(low[rows:]).astype(f32)
        return take_share(summed) + tp_swap(give_share(summed).astype(bf16)).astype(f32)

    pick = (
        jnp.arange(8, dtype=jnp.int32)[:, None] == jnp.arange(128, dtype=jnp.int32)[None, :]
    ).astype(bf16)
    post_rows = matmul_rt(pick, attn_grid[:, a_cols + q_cols :])
    post_attn, post_mlp = post_rows[0:1], post_rows[1:2]
    branch_partial = matmul_rt(tie(attn_out, down_held), out_w)
    branch_core = branch_partial[:rows] + core_swap(branch_partial[rows:].astype(bf16)).astype(f32)
    branch_give = give_share(branch_core).astype(bf16)
    branch_got = tp_swap(branch_give)
    gate_w = spread_end(tie(gate_every, branch_give))
    branch = take_share(branch_core) + tie(branch_got, gate_w).astype(f32)
    up_w = spread_end(up_every)

    normal_two, inverse_two = norm_parts(branch)
    middle = take_share(residual) + normal_two * post_attn
    normal_three, inverse_three = norm_parts(middle)

    three_low = normal_three.astype(bf16)
    down_w = spread_end(tie(down_every, three_low))

    def ring_rows(own, step_fn, before_last=None, own_first=False):
        sums = []
        chunk = own
        for step in range(z_size):
            if step:
                chunk = z_shift(chunk, 1)
            if step == 1 and own_first:
                chunk = tie(chunk, partial)
            both = jnp.concatenate([chunk, core_swap(chunk)], axis=0)
            partial = step_fn(step, both)
            sums.append(
                partial[:share] + core_swap(partial[share:].astype(bf16)).astype(f32)
            )
        total, lows = sums[1], []
        for step in list(range(2, z_size)) + [0]:
            lows.append(total.astype(bf16))
            if step == 0 and before_last is not None:
                lows[-1] = tie(lows[-1], before_last())
            total = z_shift(lows[-1], 1).astype(f32) + sums[step]
        return total, lows

    mlp_in, gates, ups, inners = {}, {}, {}, {}

    def mlp_forward(step, both):
        mlp_in[step] = both
        gates[step] = matmul(both, gate_w)
        ups[step] = matmul(both, up_w)
        inners[step] = (jax.nn.gelu(gates[step], approximate=True) * ups[step]).astype(bf16)
        return matmul_rt(inners[step], down_w)

    mlp_share, _ = ring_rows(three_low, mlp_forward)

    normal_four, inverse_four = norm_parts(mlp_share)
    cont_live = (
        (jnp.arange(cont_size, dtype=jnp.int32)[None, :] < cont_len[:, None])
        .astype(f32)
        .reshape(cont_rows)
    )
    live_rows = jnp.concatenate([jnp.ones((prompt_local,), f32), cont_live])
    live = take_share(live_rows)[:, None]
    result_share = ((middle + normal_four * post_mlp) * live).astype(bf16)
    result_rows = rows_of(result_share, tp_swap(result_share))
    cot_rows = jnp.concatenate(
        [prompt_cot.reshape(prompt_local, width), cont_cot.reshape(cont_rows, width)], axis=0
    )
    grad_result = take_share(cot_rows).astype(f32) * live
    grad_post_mlp = jnp.sum(grad_result * normal_four, axis=0)
    grad_mlp = norm_back(grad_result * post_mlp, normal_four, inverse_four)

    grad_outs, grad_gates, grad_ups = {}, {}, {}

    def mlp_backward(step, both):
        grad_outs[step] = both
        grad_inner = matmul(both, down_w)
        pull = jax.vjp(
            lambda gate_in, up_in: jax.nn.gelu(gate_in, approximate=True) * up_in,
            gates[step],
            ups[step],
        )[1]
        grad_gate, grad_up = pull(grad_inner)
        grad_gates[step] = grad_gate.astype(bf16)
        grad_ups[step] = grad_up.astype(bf16)
        return matmul_rt(grad_gates[step], gate_w) + matmul_rt(grad_ups[step], up_w)

    def blocks_back(got):
        return jnp.concatenate([got[i] for i in range(z_size)], axis=1).astype(f32)

    def reduce_terms(full):
        full = full.reshape(z_size, y_size, 2, part, block)

        def of_core(which):
            return lax.dynamic_slice_in_dim(full, which, 1, 2)[:, :, 0].transpose(1, 0, 2, 3)

        halves = by_core(of_core(core), core_swap(of_core(1 - core)))
        return jnp.stack(halves, axis=1).reshape((y_size * 2 * z_size,) + full.shape[3:])

    def reduce(every):
        return lax.psum_scatter(
            every, ("ctx", "tp"), scatter_dimension=0, tiled=True, axis_index_groups=same_core
        )

    def joined(pieces):
        return jnp.concatenate([pieces[step] for step in range(z_size)], axis=0)

    down_terms = []

    def before_last():
        grad_down_w = matmul_lt(joined(grad_outs), joined(inners)).astype(bf16)
        down_terms.append(reduce_terms(grad_down_w))
        return down_terms[0]

    grad_three, lows = ring_rows(grad_mlp.astype(bf16), mlp_backward, before_last, True)
    down_sum = reduce(down_terms[0])
    all_in = joined(mlp_in)
    grad_gate_w = matmul_lt(tie(all_in, lows[2]), joined(grad_gates)).astype(bf16)
    gate_terms = reduce_terms(grad_gate_w)
    gate_sum = reduce(gate_terms)
    grad_three = tie(grad_three, grad_gate_w)

    grad_middle = grad_result + norm_back(grad_three, normal_three, inverse_three)
    grad_post_attn = jnp.sum(grad_middle * normal_two, axis=0)
    grad_branch = norm_back(grad_middle * post_attn, normal_two, inverse_two).astype(bf16)
    grad_up_w = matmul_lt(tie(all_in, grad_branch), joined(grad_ups)).astype(bf16)
    up_terms = reduce_terms(grad_up_w)
    up_sum = reduce(up_terms)
    down_got = over_z(tie(down_sum, grad_branch))
    branch_rows = rows_of(grad_branch, tie(tp_swap(grad_branch), grad_up_w, down_got))
    post_terms = jnp.stack([grad_post_attn, grad_post_mlp], axis=0)
    post_terms = post_terms.reshape(2, z_size, y_size, 2, part).transpose(1, 2, 3, 0, 4)
    post_y = scatter_y(post_terms)
    branch_rows = tie(branch_rows, post_y)
    post_z = scatter_z(post_y)
    branch_chip = jnp.concatenate([branch_rows, core_swap(branch_rows)], axis=0)
    grad_attn = matmul(branch_chip, out_w).astype(bf16)
    grad_out_w = matmul_lt(tie(branch_chip, grad_attn), attn_out).astype(bf16)
    out_y = scatter_y(grad_out_w.reshape(z_size, y_size, 2 * part, q_cols)).astype(bf16)
    grad_heads = jnp.stack(
        [grad_attn[:, i * HD : (i + 1) * HD] for i in range(shared_by)], axis=0
    ).reshape(shared_by, 2, rows, HD)
    prompt_gq, prompt_gk, prompt_gv = attend_backward(
        prompt_query,
        own_kv[:, :HD],
        own_kv[:, HD:],
        prompt_allowed,
        prompt_total,
        grad_heads[:, :, :prompt_local].reshape(-1, HD),
    )
    prompt_gkv = jnp.concatenate([prompt_gk, prompt_gv], axis=1)
    gate_got = over_z(tie(gate_sum, grad_attn))
    grad_heads = tie(grad_heads, gate_got, *post_z)
    cont_gq, cont_gkv, own_gkv = [], [], []
    for i in range(2 * cont_count):
        at = prompt_local + (i % cont_count) * cont_size
        half = i // cont_count
        query, kv, _, total = conts[i]
        gq, gk, gv = attend_backward(
            query,
            kv[:, :HD],
            kv[:, HD:],
            cont_allowed,
            total,
            grad_heads[:, half, at : at + cont_size].reshape(-1, HD),
        )
        cont_gq.append(gq.reshape(shared_by, cont_size, HD))
        gkv = jnp.concatenate([gk, gv], axis=1)
        cont_gkv.append(gkv[:span])
        own_gkv.append(gkv[span:])

    def kv_take(z_at, y_at):
        length = 2 * prompt_local

        def piece(values):
            return lax.dynamic_slice_in_dim(values, y_at * length, length, 0)

        total = jnp.where(z_at == z, piece(prompt_gkv), 0.0)
        for which, term in zip(which_prompt, cont_gkv):
            total = total + jnp.where(z_at == which, piece(term), 0.0)
        return total

    out_got = over_z(out_y)
    up_got = over_z(tie(up_sum, out_got))
    kv_terms, kv_total = scatter_grid(kv_take, pairs, (out_y, up_got))
    grad_q = rows_order(prompt_gq.reshape(shared_by, 2, prompt_local, HD), cont_gq)
    grad_q_proj = jnp.concatenate(
        [
            rotary(grad_q[:, i * HD : (i + 1) * HD] * query_scale, cosine, -sine_wave)
            for i in range(shared_by)
        ],
        axis=1,
    ).astype(bf16)
    grad_q_w = matmul_lt(chip_rows, grad_q_proj).astype(bf16)
    q_y = scatter_y(tie(grad_q_w, kv_total).reshape(z_size, y_size, 2 * part, q_cols))
    kv_low = add_up(tie(kv_terms, q_y))
    kv_sum = kv_low.reshape(2, prompt_local, 2 * HD)
    halves = []
    for half in range(2):
        halves.append(kv_sum[half])
        halves.extend(own_gkv[half * cont_count : (half + 1) * cont_count])
    grad_kv = jnp.concatenate(halves, axis=0)
    grad_kv_proj = jnp.concatenate(
        [rotary(grad_kv[:, :HD], cosine, -sine_wave), grad_kv[:, HD:]], axis=1
    ).astype(bf16)
    one_partial = matmul_rt(grad_q_proj, attn_w[:, :q_cols]) + matmul_rt(
        grad_kv_proj, attn_w[:, q_cols:]
    )
    one_core = one_partial[:rows] + core_swap(one_partial[rows:].astype(bf16)).astype(f32)
    one_give = give_share(one_core).astype(bf16)
    one_got = tp_swap(one_give)
    grad_kv_w = matmul_lt(tie(chip_rows, one_give), grad_kv_proj).astype(bf16)
    kvw_y = scatter_y(grad_kv_w.reshape(z_size, y_size, 2 * part, 2 * kv_cols))
    q_got = over_z(tie(q_y, one_give).astype(bf16))
    one_got = tie(one_got, q_got)
    grad_one = take_share(one_core) + one_got.astype(f32)
    grad_input = grad_middle + norm_back(grad_one, take_share(normal_one), take_share(inverse_one))
    input_low = grad_input.astype(bf16)
    kvw_got = over_z(kvw_y.astype(bf16))
    raw_down = blocks_back(tie(down_got, input_low))
    raw_gate = blocks_back(tie(gate_got, input_low))
    raw_up = blocks_back(tie(up_got, input_low))
    out_sum = jnp.sum(tie(out_got, input_low).astype(f32), axis=0)
    q_sum = jnp.sum(tie(q_got, input_low).astype(f32), axis=0)
    kvw_sum = jnp.sum(tie(kvw_got, input_low).astype(f32), axis=0)
    post_sum = add_up(post_z)
    input_rows = rows_of(input_low, tp_swap(input_low)).astype(f32)

    def split_core(summed):
        mine = lax.dynamic_slice_in_dim(summed, core * part, part, 0)
        give = lax.dynamic_slice_in_dim(summed, (1 - core) * part, part, 0).astype(bf16)
        return mine, core_swap(give).astype(f32)

    grad_out = jnp.concatenate(by_core(*split_core(out_sum)), axis=1).T
    post_sum = row_of(post_sum, core) + core_swap(row_of(post_sum, 1 - core))
    raw_q = jnp.concatenate(by_core(*split_core(q_sum)), axis=1)
    first, second = by_core(*split_core(kvw_sum))
    raw_k = jnp.concatenate([first[:, :kv_cols], second[:, :kv_cols]], axis=1)
    raw_v = jnp.concatenate([first[:, kv_cols:], second[:, kv_cols:]], axis=1)

    def gain_sum(raw, weight):
        return jnp.sum(raw * weight.astype(f32), axis=1)

    gain_terms = jnp.stack(
        [
            gain_sum(raw_q, w_query) + gain_sum(raw_k, w_key) + gain_sum(raw_v, w_value),
            post_sum[0],
            gain_sum(raw_gate, w_gate) + gain_sum(raw_up, w_up),
            post_sum[1],
        ],
        axis=0,
    )
    gain_grads = gain_terms + tp_swap(gain_terms)

    return (
        result_rows[:prompt_local].reshape(1, prompt_local, width),
        result_rows[prompt_local:].reshape(cont_count, cont_size, width),
        input_rows[:prompt_local].reshape(1, prompt_local, width),
        input_rows[prompt_local:].reshape(cont_count, cont_size, width),
        gain_grads[0],
        gain_grads[1],
        gain_grads[2],
        gain_grads[3],
        raw_q * gain_one,
        raw_k * gain_one,
        raw_v * gain_one,
        grad_out,
        raw_gate * gain_three,
        raw_up * gain_three,
        raw_down.T,
    )


def solution(mesh):
    in_specs = (
        P("fsdp", "ctx", None),
        P(("fsdp", "ctx"), None, None),
        P(("fsdp", "ctx")),
        P(("fsdp", "ctx")),
        P(("fsdp", "ctx")),
        P(("fsdp", "ctx")),
        P(("fsdp", "ctx")),
        P(("fsdp", "ctx")),
        P(("fsdp", "ctx"), "tp"),
        P(("fsdp", "ctx"), "tp"),
        P(("fsdp", "ctx"), "tp"),
        P("tp", ("fsdp", "ctx")),
        P(("fsdp", "ctx"), "tp"),
        P(("fsdp", "ctx"), "tp"),
        P("tp", ("fsdp", "ctx")),
        P("fsdp", "ctx", None),
        P(("fsdp", "ctx"), None, None),
    )
    out_specs = (
        P("fsdp", "ctx", None),
        P(("fsdp", "ctx"), None, None),
        P("fsdp", "ctx", None),
        P(("fsdp", "ctx"), None, None),
        P(("fsdp", "ctx")),
        P(("fsdp", "ctx")),
        P(("fsdp", "ctx")),
        P(("fsdp", "ctx")),
        P(("fsdp", "ctx"), "tp"),
        P(("fsdp", "ctx"), "tp"),
        P(("fsdp", "ctx"), "tp"),
        P("tp", ("fsdp", "ctx")),
        P(("fsdp", "ctx"), "tp"),
        P(("fsdp", "ctx"), "tp"),
        P("tp", ("fsdp", "ctx")),
    )
    return jax.shard_map(shards, mesh=mesh, in_specs=in_specs, out_specs=out_specs, check_vma=False)
```
